128 devices in a mesh: wide: 8 (over y, core), narrow: 16 (over x, z).
Axes of the slice: x: 4, y: 4, z: 4, core: 2. Of those that a mesh axis runs over, the one named last changes fastest.
Arguments:
- site_basis: bfloat16 [512, 512], P(('wide', 'narrow')), may hold values from -0.25 to 0.25
- left_ops: bfloat16 [384, 512, 512], P(('wide', 'narrow')), may hold values from -0.25 to 0.25
- right_ops: bfloat16 [384, 512, 512], P(('wide', 'narrow')), may hold values from -0.25 to 0.25
- integrals: bfloat16 [384, 384], replicated, may hold values from -0.3125 to 0.3125
- wavefunction: bfloat16 [512, 512], P(('wide', 'narrow')), may hold values from -6 to 6
- pair_order: int32 [384], replicated, may hold values from 0 to 383, each once
- sector_sizes: int32 [8], replicated, may hold values from 1 to 128, 512 in all
Outputs:
- propagated: float32 [512, 512], P(('wide', 'narrow'))
The draws below stay inside these ranges and needn't reach their ends.
Inputs may be any that keep to these rules, and one draw needn't show every extreme that they name: `pair_order`: each orbital pair stands in exactly one of the 384 slots. `sector_sizes`: the sizes sum to 512.
All inputs are finite; a program needn't handle non-finite values.
Results may differ from the reference program's by a relative error of at most 0.008.
Values may be sent and summed in bfloat16 or wider, within the bound.
A program may use at most 64 MiB of HBM per device.

```python
import math
import jax
import jax.numpy as jnp
import numpy as np
from jax import lax

M = 512
ORDER = 3
BLOCKS = 8
PAIRS = 384


def steps_of(rng, shape, split, low, largest):
    gain = 1.0
    for dim, shards_of in split:
        steps = jax.random.uniform(jax.random.fold_in(jax.random.fold_in(rng, 6), dim), (shards_of,), jnp.float32, low / len(split), largest / len(split))
        gain = gain * jnp.repeat(jnp.exp(steps), shape[dim] // shards_of).reshape((-1,) + (1,) * (len(shape) - 1 - dim))
    return gain


def length_profile(count, total, reach, slope):
    weights = [(1 << 20) // math.isqrt(grade ** slope) + 1 for grade in range(2, count + 1)]
    surplus, holding = total - reach - (count - 1), [1] * (count - 1)
    while surplus > 0:
        movable = [i for i in range(count - 1) if holding[i] < reach]
        mass, remaining = sum([weights[i] for i in movable]), surplus
        for i in movable:
            addition = min(reach - holding[i], max(1, remaining * weights[i] // mass), surplus)
            holding[i] = holding[i] + addition
            surplus = surplus - addition
    return np.array([reach] + holding)


def ragged(own_key, number_of, total, reach, skew):
    if number_of == 2:
        one = jax.random.randint(own_key, (), max(1, total - reach), min(reach, total - 1) + 1)
        return jnp.stack([one, total - one])
    tallies = jnp.asarray(length_profile(number_of, total, reach, skew), jnp.int32)
    twos = (number_of - 1) // 2
    source_of, taker = tallies[1:1 + 2 * twos:2], tallies[2:2 + 2 * twos:2]
    slack = jnp.minimum(source_of - 1, reach - taker)
    moved = jax.random.randint(jax.random.fold_in(own_key, 1), (twos,), 0, 1 << 20) % (slack + 1)
    tallies = tallies.at[1:1 + 2 * twos:2].set(source_of - moved).at[2:2 + 2 * twos:2].set(taker + moved)
    return tallies[jax.random.permutation(jax.random.fold_in(own_key, 2), number_of)]


def bell_draw(own_key, dims, spread, bound, split=(), kind=jnp.bfloat16):
    result = jax.random.normal(own_key, dims, jnp.float32) * spread
    if len(split) > 0:
        result = steps_of(own_key, dims, split, -0.22, 0.18) * result
    return jnp.clip(result, min=-bound, max=bound).astype(kind)


def setup_inputs(seed: int = 0) -> dict:
    arg_keys = jax.random.split(jax.random.key(seed), 8)
    site_basis = bell_draw(arg_keys[0], (M, M), M ** -0.5, 0.25, ((0, 128),))
    left_ops = bell_draw(arg_keys[1], (PAIRS, M, M), M ** -0.5, 0.25, ((0, 128),))
    right_ops = bell_draw(arg_keys[2], (PAIRS, M, M), M ** -0.5, 0.25, ((0, 128),))
    integrals = bell_draw(arg_keys[3], (PAIRS, PAIRS), PAIRS ** -0.5, 0.3125)
    wavefunction = bell_draw(arg_keys[4], (M, M), 1.0, 6.0, ((0, 128),))
    pair_order = jax.random.permutation(arg_keys[5], PAIRS).astype(jnp.int32)
    sector_sizes = ragged(arg_keys[6], BLOCKS, M, M // 4, 2).astype(jnp.int32)
    return dict(site_basis=site_basis, left_ops=left_ops, right_ops=right_ops, integrals=integrals, wavefunction=wavefunction, pair_order=pair_order, sector_sizes=sector_sizes)


def sector_mask(sector_sizes, row_ids, col_ids):
    block_ends = jnp.cumsum(sector_sizes).astype(jnp.int32)
    row_block = lax.optimization_barrier(jnp.sum((row_ids[:, None] >= block_ends[None, :]).astype(jnp.int32), axis=1))
    col_block = lax.optimization_barrier(jnp.sum((col_ids[:, None] >= block_ends[None, :]).astype(jnp.int32), axis=1))
    return (jnp.abs(row_block[:, None] - col_block[None, :]) <= 2).astype(jnp.float32)

def product(left, right):
    return jnp.dot(left.astype(jnp.float32), right.astype(jnp.float32), precision=lax.Precision.HIGHEST)

def reference(site_basis, left_ops, right_ops, integrals, wavefunction, pair_order, sector_sizes):

    def build(left_one):
        rotated = product(left_one, site_basis).astype(jnp.bfloat16)
        return product(site_basis.T, rotated).astype(jnp.bfloat16)
    built_ops = lax.map(build, left_ops)
    mixing = jnp.take(jnp.take(integrals, pair_order, axis=0), pair_order, axis=1)
    comp_ops = product(mixing, right_ops.reshape(PAIRS, M * M))
    comp_ops = comp_ops.astype(jnp.bfloat16).reshape(PAIRS, M, M)
    states = jnp.arange(M, dtype=jnp.int32)
    masking = sector_mask(sector_sizes, states, states)
    state = (wavefunction.astype(jnp.float32) * masking).astype(jnp.bfloat16)
    summed = state.astype(jnp.float32)
    step_size = 2.0 / math.sqrt(PAIRS)
    for order_index in range(1, ORDER + 1):

        def accumulate(carry, pair_ops, current=state):
            left_one, right_one = pair_ops
            applied = product(left_one, current).astype(jnp.bfloat16)
            return (carry + product(applied, right_one.T), None)
        full_term, _ = lax.scan(accumulate, jnp.zeros((M, M), jnp.float32), (built_ops, comp_ops))
        state = (-(step_size / order_index) * masking * full_term).astype(jnp.bfloat16)
        summed = summed + state.astype(jnp.float32)
    return summed
```

```python
import math

import jax
import jax.numpy as jnp
from jax import lax
from jax.experimental import pallas as pl
from jax.experimental.pallas import tpu as pltpu
from jax.sharding import PartitionSpec as P

ORDER = 3
ROWS, LANES = 16, 128
BF16, F32 = jnp.bfloat16, jnp.float32
BOTH = ("wide", "narrow")
MESH = pl.DeviceIdType.MESH


def dot(a, b, dims=((1,), (0,))):
    return lax.dot_general(a, b, (dims, ((), ())), preferred_element_type=F32)


def iota(shape, dim):
    return lax.broadcasted_iota(jnp.int32, shape, dim)


def tile_swap(size):
    o, m = iota((size, size), 0), iota((size, size), 1)
    return (m == (o & 15) * 16 + (o >> 4)).astype(F32).astype(BF16)


def row_blocks(o):
    return ((o & 63) >> 2) * 16 + (o >> 6) * 4 + (o & 3)


def kernel(
    order_ref, sizes_ref, basis_ref, left_ref, right_ref, integrals_ref, wave_ref,
    out_ref,
    left_v, pack_v, bw_v, u_v, built_v, applied_v, recv_v, bm_v, ym_v, cbuf_v, comp_v,
    mix_v, state_v, part_v, rs_v, last_v, tile_v, local_sem, send_sem, recv_sem,
    *, states, pairs, parts,
):
    per = pairs // parts
    wide, narrow = lax.axis_size("wide"), lax.axis_size("narrow")
    w, n = lax.axis_index("wide"), lax.axis_index("narrow")
    me = w * narrow + n
    across = states // LANES
    step_size = 2.0 / math.sqrt(pairs)

    def peer(k):
        p = lax.rem(me + k, parts)
        return p, (p // narrow, lax.rem(p, narrow))

    def tile_of(p):
        return (
            pl.ds(pl.multiple_of(p // across * ROWS, ROWS), ROWS),
            pl.ds(pl.multiple_of(lax.rem(p, across) * LANES, LANES), LANES),
        )

    def send_all(phase, src, dst):
        def step(k, carry):
            p, device = peer(k)
            pltpu.make_async_remote_copy(
                src_ref=src(p), dst_ref=dst, send_sem=send_sem.at[phase],
                recv_sem=recv_sem.at[phase], device_id=device, device_id_type=MESH,
            ).start()
            return carry

        lax.fori_loop(1, parts, step, 0)

    def wait_bytes(sem, phase, ref):
        pltpu.make_async_copy(ref, ref, sem.at[phase]).wait()

    barrier = pltpu.get_barrier_semaphore()

    def greet(k, carry):
        _, device = peer(k)
        pl.semaphore_signal(barrier, inc=1, device_id=device, device_id_type=MESH)
        return carry

    lax.fori_loop(1, parts, greet, 0)
    left_copy = pltpu.make_async_copy(left_ref, left_v, local_sem.at[0])
    left_copy.start()
    mine = pl.ds(me * per, per)
    mine_rows, mine_cols = tile_of(me)
    own_copy = pltpu.make_async_copy(
        right_ref.at[:, mine_rows, mine_cols], recv_v.at[mine], local_sem.at[1]
    )
    own_copy.start()

    def packed(ref):
        rows = ref[...].astype(F32)
        return jnp.concatenate(
            [rows[:, c * LANES : (c + 1) * LANES] for c in range(across)], axis=0
        ).astype(BF16)

    pack_v[0] = packed(basis_ref)
    pack_v[1] = packed(wave_ref)
    bw_v[me] = pack_v[...]

    chosen = (iota((pairs, pairs), 0) == order_ref[...]).astype(F32).astype(BF16)
    by_column = dot(integrals_ref[...], chosen).astype(BF16)
    mix_v[...] = dot(chosen, by_column, ((0,), (0,))).astype(BF16)

    ends, total = [], jnp.int32(0)
    for b in range(sizes_ref.shape[0]):
        total = total + sizes_ref[b]
        ends.append(total)

    def block_of(ids):
        found = jnp.zeros_like(ids)
        for end in ends:
            found = found + (ids >= end).astype(jnp.int32)
        return found

    def mask_of(row_ids, col_ids):
        return (jnp.abs(block_of(row_ids) - block_of(col_ids)) <= 2).astype(F32)

    pl.semaphore_wait(barrier, parts - 1)
    send_all(0, lambda p: pack_v, bw_v.at[me])
    send_all(1, lambda p: right_ref.at[(slice(None), *tile_of(p))], recv_v.at[mine])

    wait_bytes(recv_sem, 0, bw_v.at[pl.ds(0, parts - 1)])
    square = (256, 256)
    spread = (iota(square, 1) == row_blocks(iota(square, 0))).astype(F32).astype(BF16)
    gather = (iota(square, 0) == row_blocks(iota(square, 1))).astype(F32).astype(BF16)
    for g in range(states // 64):
        both = jnp.concatenate(
            [bw_v[16 * g : 16 * (g + 1), i].reshape(256, LANES) for i in range(2)], axis=1
        )
        both = dot(spread, both)
        for c in range(across):
            rows, cols = slice(64 * g, 64 * (g + 1)), slice(c * LANES, (c + 1) * LANES)
            mask = mask_of(
                64 * g + iota((64, 1), 0), c * LANES + iota((1, LANES), 1)
            )
            block = both[64 * c : 64 * (c + 1)]
            u_v[rows, cols] = block[:, :LANES].astype(BF16)
            state_v[0, rows, cols] = (block[:, LANES:] * mask).astype(BF16)

    left_copy.wait()

    def build(s, carry):
        rotated = dot(left_v[s], u_v[...]).astype(BF16)
        built_v[s] = dot(u_v[...], rotated, ((0,), (0,))).astype(BF16)
        return carry

    lax.fori_loop(0, per, build, 0)

    def apply(k):
        def one(s, carry):
            applied_v[s] = dot(built_v[s], state_v[k]).astype(BF16)
            return carry

        lax.fori_loop(0, per, one, 0)

    apply(0)

    own_copy.wait()
    wait_bytes(recv_sem, 1, recv_v.at[pl.ds(0, pairs - per)])
    swap = tile_swap(256)

    def into_rows(q, carry):
        base = pl.multiple_of(q * 32, 32)
        both = jnp.concatenate(
            [recv_v[pl.ds(base + 16 * i, 16)].reshape(256, LANES) for i in range(2)], axis=1
        )
        both = dot(swap, both).astype(BF16)
        for r in range(16):
            for i in range(2):
                bm_v[pl.ds(base + 16 * i, 16), r * LANES : (r + 1) * LANES] = both[
                    16 * r : 16 * (r + 1), i * LANES : (i + 1) * LANES
                ]
        return carry

    lax.fori_loop(0, pairs // 32, into_rows, 0)

    def mix(c, carry):
        cols = pl.ds(pl.multiple_of(c * 256, 256), 256)
        ym_v[:, cols] = dot(mix_v[...], bm_v[:, cols]).astype(BF16)
        return carry

    lax.fori_loop(0, 8, mix, 0)

    def into_tiles(q, carry):
        base = pl.multiple_of(q * 32, 32)
        both = jnp.concatenate(
            [
                jnp.concatenate(
                    [
                        ym_v[pl.ds(base + 16 * i, 16), r * LANES : (r + 1) * LANES]
                        for r in range(16)
                    ],
                    axis=0,
                )
                for i in range(2)
            ],
            axis=1,
        )
        both = dot(swap, both).astype(BF16)
        for i in range(2):
            cbuf_v[pl.ds(base + 16 * i, 16)] = both[:, i * LANES : (i + 1) * LANES].reshape(
                16, 16, LANES
            )
        return carry

    lax.fori_loop(0, pairs // 32, into_tiles, 0)
    send_all(2, lambda p: cbuf_v.at[pl.ds(p * per, per)], comp_v.at[:, mine_rows, mine_cols])
    comp_v[:, mine_rows, mine_cols] = cbuf_v[mine]
    wait_bytes(recv_sem, 2, cbuf_v.at[pl.ds(0, pairs - per)])

    def term():
        def one(i, carry):
            rows = pl.ds(pl.multiple_of(i * 256, 256), 256)
            total = dot(applied_v[0, rows, :], comp_v[0], ((1,), (1,)))
            for s in range(1, per):
                total += dot(applied_v[s, rows, :], comp_v[s], ((1,), (1,)))
            part_v[rows, :] = total.astype(BF16)
            return carry

        lax.fori_loop(0, states // 256, one, 0)

    def summed(slot):
        def some(j, carry):
            return carry + jnp.sum(rs_v[slot, pl.ds(j * 8, 8)].astype(F32), axis=0)

        return lax.fori_loop(0, parts // 8, some, jnp.zeros((ROWS, LANES), F32))

    tiles = parts - 1
    for k in range(1, ORDER):
        term()
        slot = k - 1
        send_all(1 + 2 * k, lambda p: part_v.at[tile_of(p)], rs_v.at[slot, me])
        rs_v[slot, me] = part_v[mine_rows, mine_cols]
        mask = mask_of(
            me // across * ROWS + iota((ROWS, 1), 0),
            lax.rem(me, across) * LANES + iota((1, LANES), 1),
        )
        factor = -(step_size / k)
        wait_bytes(recv_sem, 1 + 2 * k, rs_v.at[slot, pl.ds(0, tiles)])
        new = (factor * mask * summed(slot)).astype(BF16)
        tile_v[slot] = new
        state_v[k, mine_rows, mine_cols] = new
        send_all(2 + 2 * k, lambda p: tile_v.at[slot], state_v.at[(k, mine_rows, mine_cols)])
        wait_bytes(send_sem, 1 + 2 * k, rs_v.at[slot, pl.ds(0, tiles)])
        wait_bytes(recv_sem, 2 + 2 * k, rs_v.at[slot, pl.ds(0, tiles)])
        apply(k)

    term()
    for g in range(states // 64):
        stacked = jnp.concatenate(
            [
                part_v[64 * g : 64 * (g + 1), c * LANES : (c + 1) * LANES]
                for c in range(across)
            ],
            axis=0,
        )
        last_v[16 * g : 16 * (g + 1)] = dot(gather, stacked).astype(BF16).reshape(16, 16, LANES)
    slot, phase = ORDER - 1, 1 + 2 * ORDER
    send_all(phase, lambda p: last_v.at[p], rs_v.at[slot, me])
    rs_v[slot, me] = last_v[me]
    own_rows = states // parts
    pick = (iota((8, states), 1) == own_rows * me + iota((8, states), 0)).astype(F32).astype(BF16)
    so_far = dot(pick, state_v[0])
    for k in range(1, ORDER):
        so_far += dot(pick, state_v[k])
    wait_bytes(recv_sem, phase, rs_v.at[slot, pl.ds(0, tiles)])
    total = summed(slot)
    for c in range(across):
        mask = mask_of(
            own_rows * me + iota((own_rows, 1), 0), c * LANES + iota((1, LANES), 1)
        )
        new = -(step_size / ORDER) * mask * total[own_rows * c : own_rows * (c + 1)]
        cols = slice(c * LANES, (c + 1) * LANES)
        out_ref[:, cols] = so_far[:own_rows, cols] + new.astype(BF16).astype(F32)

    wait_bytes(send_sem, 0, bw_v.at[pl.ds(0, tiles)])
    wait_bytes(send_sem, 1, recv_v.at[pl.ds(0, pairs - per)])
    wait_bytes(send_sem, 2, recv_v.at[pl.ds(0, pairs - per)])
    for k in range(1, ORDER):
        wait_bytes(send_sem, 2 + 2 * k, rs_v.at[slot, pl.ds(0, tiles)])
    wait_bytes(send_sem, phase, rs_v.at[slot, pl.ds(0, tiles)])


def local(site_basis, left_ops, right_ops, integrals, wavefunction, pair_order, sector_sizes):
    states = wavefunction.shape[1]
    pairs = integrals.shape[0]
    per = left_ops.shape[0]
    parts = pairs // per
    vmem = pl.BlockSpec(memory_space=pltpu.VMEM)
    anywhere = pl.BlockSpec(memory_space=pl.ANY)
    ops = (per, states, states)
    phases = 2 + 2 * ORDER
    body = lambda *refs: kernel(*refs, states=states, pairs=pairs, parts=parts)
    return pl.pallas_call(
        body,
        out_shape=jax.ShapeDtypeStruct(wavefunction.shape, F32),
        in_specs=[
            vmem, pl.BlockSpec(memory_space=pltpu.SMEM), vmem, anywhere, anywhere, vmem, vmem
        ],
        out_specs=vmem,
        scratch_shapes=[
            pltpu.VMEM(ops, BF16),
            pltpu.VMEM((2, ROWS, LANES), BF16),
            pltpu.VMEM((parts, 2, ROWS, LANES), BF16),
            pltpu.VMEM((states, states), BF16),
            pltpu.VMEM(ops, BF16),
            pltpu.VMEM(ops, BF16),
            pltpu.VMEM((pairs, ROWS, LANES), BF16),
            pltpu.VMEM((pairs, ROWS * LANES), BF16),
            pltpu.VMEM((pairs, ROWS * LANES), BF16),
            pltpu.VMEM((pairs, ROWS, LANES), BF16),
            pltpu.VMEM(ops, BF16),
            pltpu.VMEM((pairs, pairs), BF16),
            pltpu.VMEM((ORDER, states, states), BF16),
            pltpu.VMEM((states, states), BF16),
            pltpu.VMEM((ORDER, parts, ROWS, LANES), BF16),
            pltpu.VMEM((parts, ROWS, LANES), BF16),
            pltpu.VMEM((ORDER, ROWS, LANES), BF16),
            pltpu.SemaphoreType.DMA((2,)),
            pltpu.SemaphoreType.DMA((phases,)),
            pltpu.SemaphoreType.DMA((phases,)),
        ],
        compiler_params=pltpu.CompilerParams(
            collective_id=0, has_side_effects=True, vmem_limit_bytes=48 << 20
        ),
    )(
        pair_order.reshape(1, pairs), sector_sizes, site_basis, left_ops, right_ops,
        integrals, wavefunction,
    )


def solution(mesh):
    in_specs = (
        P(BOTH, None), P(BOTH, None, None), P(BOTH, None, None), P(), P(BOTH, None), P(), P()
    )
    return jax.shard_map(
        local, mesh=mesh, in_specs=in_specs, out_specs=P(BOTH, None), check_vma=False
    )
```

```python
import math

import jax
import jax.numpy as jnp
from jax import lax
from jax.experimental import pallas as pl
from jax.experimental.pallas import tpu as pltpu
from jax.sharding import PartitionSpec as P

ORDER = 3
ROWS, LANES = 16, 128
BF16, F32 = jnp.bfloat16, jnp.float32
BOTH = ("wide", "narrow")
MESH = pl.DeviceIdType.MESH


def dot(a, b, dims=((1,), (0,))):
    return lax.dot_general(a, b, (dims, ((), ())), preferred_element_type=F32)


def iota(shape, dim):
    return lax.broadcasted_iota(jnp.int32, shape, dim)


def tile_swap(size):
    o, m = iota((size, size), 0), iota((size, size), 1)
    return (m == (o & 15) * 16 + (o >> 4)).astype(F32).astype(BF16)


def spread_row(o):
    return ((o & 63) >> 2) * 16 + (o >> 6) * 4 + (o & 3)


def gather_row(o):
    return ((o >> 2) & 1) * 128 + ((o >> 3) & 1) * 64 + (o >> 4) * 4 + (o & 3)


def far_first(depth):
    steps = [
        (dy, dx, dz) for dy in range(4) for dx in range(4) for dz in range(depth)
    ]
    hops = lambda d: min(d[0], 4 - d[0]) + min(d[1], 4 - d[1])
    along_z = lambda d: min(d[2], 4 - d[2]) if depth == 4 else 2 * d[2]
    return sorted(steps, key=lambda d: -hops(d) - along_z(d))


def kernel(
    order_ref, sizes_ref, basis_ref, left_ref, right_ref, integrals_ref, wave_ref,
    out_ref,
    order_v, sizes_v, basis_v, integrals_v, wave_v,
    left_v, pack_v, bw_v, u_v, built_v, applied_v, recv_v, bm_v, ym_v, cbuf_v, comp_v,
    mix_v, state_v, part_v, rs_v, last_v, tile_v, swap_v, pair_v, other_v, acc_v, local_sem, send_sem, recv_sem,
    *, states, pairs, parts,
):
    per = pairs // parts
    phases = 6 + 3 * ORDER
    group = 2 * per
    narrow = lax.axis_size("narrow")
    w, n = lax.axis_index("wide"), lax.axis_index("narrow")
    core = lax.rem(w, 2)
    me = w * narrow + n
    chips = parts // 2
    chip = w // 2 * narrow + n
    partner = (w + 1 - 2 * core, n)
    across = states // LANES
    half = states // 2
    step_size = 2.0 / math.sqrt(pairs)

    y, x, z = w // 2, n // 4, lax.rem(n, 4)

    to_w = [lax.rem(y + d, 4) * 2 + core for d in range(4)]
    to_y = [lax.rem(y + d, 4) * narrow for d in range(4)]
    to_x = [lax.rem(x + d, 4) * 4 for d in range(4)]
    to_z = [lax.rem(z + d, 4) for d in range(4)]

    def block(row, col):
        return (
            pl.ds(pl.multiple_of(row * ROWS, ROWS), ROWS),
            pl.ds(pl.multiple_of(col * LANES, LANES), LANES),
        )

    def mix_block(q):
        return block(lax.div(q, across), lax.rem(q, across))

    def term_block(q):
        return block(lax.rem(q, 2) * (chips // 4) + lax.div(q, 4), lax.div(lax.rem(q, 4), 2))

    def mix_slots(q):
        return pl.ds((lax.rem(q, 2) * (chips // 2) + lax.div(q, 2)) * group, group)

    def send(phase, src, dst, device):
        pltpu.make_async_remote_copy(
            src_ref=src, dst_ref=dst, send_sem=send_sem.at[phase],
            recv_sem=recv_sem.at[phase], device_id=device, device_id_type=MESH,
        ).start()

    def each_chip(visit):
        to_n = [[i + j for j in to_z] for i in to_x]
        for dy, dx, dz in far_first(4):
            if (dy, dx, dz) != (0, 0, 0):
                visit(to_y[dy] + to_n[dx][dz], (to_w[dy], to_n[dx][dz]))

    def send_chips(phase, src, dst):
        each_chip(lambda q, device: send(phase, src(q), dst, device))

    def send_half(phase, parity, src, dst):
        first = lax.rem(parity + z, 2)
        to_n = [[i + lax.rem(z + first + 2 * j, 4) for j in range(2)] for i in to_x]
        for dy, dx, dz in far_first(2):
            q, device = to_y[dy] + to_n[dx][dz], (to_w[dy], to_n[dx][dz])
            if (dy, dx, dz) == (0, 0, 0):

                @pl.when(first == 1)
                def _():
                    send(phase, src(q), dst, device)

            else:
                send(phase, src(q), dst, device)

    def wait_bytes(sem, phase, ref):
        pltpu.make_async_copy(ref, ref, sem.at[phase]).wait()

    barrier = pltpu.get_barrier_semaphore()

    def greet(device):
        pl.semaphore_signal(barrier, inc=1, device_id=device, device_id_type=MESH)

    greet(partner)
    each_chip(lambda q, device: greet(device))
    half_rows = half // ROWS
    own_half = pl.ds(pl.multiple_of(core * half, half), half)
    other_half = pl.ds(pl.multiple_of((1 - core) * half, half), half)
    own_slots = pl.ds(core * (pairs // 2) + chip * per, per)
    other_slots = pl.ds((1 - core) * (pairs // 2) + chip * per, per)
    mix_rows, mix_cols = mix_block(chip)
    term_rows, term_cols = term_block(chip)
    loads = [
        pltpu.make_async_copy(src, dst, local_sem.at[i])
        for i, (src, dst) in enumerate(
            [
                (order_ref, order_v), (sizes_ref, sizes_v), (integrals_ref, integrals_v),
                (basis_ref, basis_v), (wave_ref, wave_v),
                (right_ref.at[:, block(core * half_rows + chip // across, 0)[0], mix_cols],
                 recv_v.at[own_slots]),
                (left_ref, left_v.at[pl.ds(core * per, per)]),
            ]
        )
    ]
    for load in loads:
        load.start()
    for load in loads[:5]:
        load.wait()

    def packed(ref):
        rows = ref[...].astype(F32)
        return jnp.concatenate(
            [rows[:, c * LANES : (c + 1) * LANES] for c in range(across)], axis=0
        ).astype(BF16)

    pack_v[0] = packed(basis_v)
    pack_v[1] = packed(wave_v)
    bw_v[core, chip] = pack_v[...]
    swap_v[...] = tile_swap(256)

    def take(ids, width):
        return (iota((pairs, width), 0) == ids).astype(F32).astype(BF16)

    def slot(of_chip, of_core, j):
        return ((of_chip // narrow * 2 + of_core) * narrow + (of_chip & (narrow - 1))) * per + j

    chosen = take(order_v[...], pairs)
    place = iota((1, pairs), 1)
    owner = (place * (65536 // group + 1)) >> 16
    rest = place - owner * group
    of_core = (rest >= per).astype(jnp.int32)
    owner = (owner & (chips // 2 - 1)) * 2 + owner // (chips // 2)
    by_row = dot(chosen, take(slot(owner, of_core, rest - of_core * per), pairs)).astype(BF16)
    place = iota((1, pairs // 2), 1)
    sender = (place * (65536 // per + 1)) >> 16
    for c in range(2):
        by_column = dot(chosen, take(slot(sender, c, place - sender * per), pairs // 2))
        by_column = dot(integrals_v[...], by_column.astype(BF16)).astype(BF16)
        mix_v[c] = dot(by_row, by_column, ((0,), (0,))).astype(BF16)

    ends, total = [], jnp.int32(0)
    for b in range(sizes_ref.shape[0]):
        total = total + sizes_v[b]
        ends.append(total)

    def block_of(ids):
        found = jnp.zeros_like(ids)
        for end in ends:
            found = found + (ids >= end).astype(jnp.int32)
        return found

    def mask_of(row_ids, col_ids):
        return (jnp.abs(block_of(row_ids) - block_of(col_ids)) <= 2).astype(F32)

    pl.semaphore_wait(barrier, chips)

    send(phases - 1, right_ref.at[:, other_half, :], other_v, partner)
    send_chips(
        1,
        lambda q: right_ref.at[
            (slice(None), *block(core * half_rows + lax.div(q, across), lax.rem(q, across)))
        ],
        recv_v.at[own_slots],
    )
    wait_bytes(recv_sem, phases - 1, other_v)
    send_chips(phases - 2, lambda q: other_v.at[(slice(None), *mix_block(q))], recv_v.at[other_slots])
    recv_v[other_slots] = other_v[:, mix_rows, mix_cols]
    send_chips(0, lambda q: pack_v, bw_v.at[core, chip])
    left_mine = left_v.at[pl.ds(core * per, per)]
    send(3, left_ref, left_mine, partner)

    def into_rows(c):
        def some(q, carry):
            base = pl.multiple_of(q * 32, 32)
            both = jnp.concatenate(
                [
                    recv_v[pl.ds(c * (pairs // 2) + base + 16 * i, 16)].reshape(256, LANES)
                    for i in range(2)
                ],
                axis=1,
            )
            both = dot(swap_v[...], both).astype(BF16)
            for r in range(16):
                for i in range(2):
                    bm_v[c, pl.ds(base + 16 * i, 16), r * LANES : (r + 1) * LANES] = both[
                        16 * r : 16 * (r + 1), i * LANES : (i + 1) * LANES
                    ]
            return carry

        lax.fori_loop(0, pairs // 64, some, 0)

    def col_chunk(j):
        return pl.ds(pl.multiple_of(j * 256, 256), 256)

    arrived = recv_v.at[pl.ds(0, (chips - 1) * per)]
    loads[5].wait()
    wait_bytes(recv_sem, 1, arrived)
    into_rows(core)

    def mix_first(j, carry):
        acc_v[:, col_chunk(j)] = dot(mix_v[core], bm_v[core, :, col_chunk(j)])
        return carry

    lax.fori_loop(0, 8, mix_first, 0)
    wait_bytes(recv_sem, phases - 2, arrived)
    into_rows(1 - core)
    for i in range(2):
        rows = slice(i * (pairs // 2), (i + 1) * (pairs // 2))

        def mix_second(j, carry, rows=rows):
            ym_v[rows, col_chunk(j)] = (
                acc_v[rows, col_chunk(j)]
                + dot(mix_v[1 - core, rows, :], bm_v[1 - core, :, col_chunk(j)])
            ).astype(BF16)
            return carry

        lax.fori_loop(0, 8, mix_second, 0)

        def into_tiles(q, carry, i=i):
            base = pl.multiple_of(q * 32 + i * (pairs // 2), 32)
            both = jnp.concatenate(
                [
                    jnp.concatenate(
                        [
                            ym_v[pl.ds(base + 16 * j, 16), r * LANES : (r + 1) * LANES]
                            for r in range(16)
                        ],
                        axis=0,
                    )
                    for j in range(2)
                ],
                axis=1,
            )
            both = dot(swap_v[...], both).astype(BF16)
            for j in range(2):
                cbuf_v[pl.ds(base + 16 * j, 16)] = both[
                    :, j * LANES : (j + 1) * LANES
                ].reshape(16, 16, LANES)
            return carry

        lax.fori_loop(0, pairs // 64, into_tiles, 0)
        send_half(
            2, i, lambda q: cbuf_v.at[mix_slots(q)], comp_v.at[:, mix_rows, mix_cols]
        )
    comp_v[:, mix_rows, mix_cols] = cbuf_v[mix_slots(chip)]

    wait_bytes(recv_sem, 0, bw_v.at[0, pl.ds(0, chips - 1)])
    send(4, bw_v.at[core], bw_v.at[core], partner)
    wait_bytes(recv_sem, 4, bw_v.at[0])
    square = (256, 256)
    spread = (iota(square, 1) == spread_row(iota(square, 0))).astype(F32).astype(BF16)
    for g in range(states // 64):
        both = jnp.concatenate(
            [
                bw_v[g % 2, g // 2 * 16 : (g // 2 + 1) * 16, i].reshape(256, LANES)
                for i in range(2)
            ],
            axis=1,
        )
        both = dot(spread, both)
        for c in range(across):
            rows, cols = slice(64 * g, 64 * (g + 1)), slice(c * LANES, (c + 1) * LANES)
            mask = mask_of(
                64 * g + iota((64, 1), 0), c * LANES + iota((1, LANES), 1)
            )
            tile = both[64 * c : 64 * (c + 1)]
            u_v[rows, cols] = tile[:, :LANES].astype(BF16)
            state_v[0, c // 2, rows, c % 2 * LANES : (c % 2 + 1) * LANES] = (
                tile[:, LANES:] * mask
            ).astype(BF16)

    loads[6].wait()
    wait_bytes(recv_sem, 3, left_mine)

    def build(s, carry):
        rotated = dot(left_v[s], u_v[...]).astype(BF16)
        built_v[s] = dot(u_v[...], rotated, ((0,), (0,))).astype(BF16)
        return carry

    lax.fori_loop(0, group, build, 0)

    def apply(k, side):
        def one(s, carry):
            applied_v[s, side] = dot(built_v[s], state_v[k, side]).astype(BF16)
            return carry

        lax.fori_loop(0, group, one, 0)

    apply(0, 0)
    apply(0, 1)
    wait_bytes(recv_sem, 2, cbuf_v.at[pl.ds(0, pairs - group)])

    def term(i):
        rows = slice(i * half, (i + 1) * half)
        total = jnp.zeros((half, half), F32)
        for s in range(group):
            for side in range(2):
                total += dot(
                    applied_v[s, side, rows, :],
                    comp_v[s, :, side * half : (side + 1) * half],
                    ((1,), (1,)),
                )
        part_v[rows, :] = total.astype(BF16)

    def summed(slot):
        def some(j, carry):
            return carry + jnp.sum(rs_v[slot, pl.ds(j * 8, 8)].astype(F32), axis=0)

        return lax.fori_loop(0, chips // 8, some, jnp.zeros((ROWS, LANES), F32))

    mask = mask_of(
        lax.rem(chip, 2) * half + chip // 4 * ROWS + iota((ROWS, 1), 0),
        core * half + lax.rem(chip, 4) // 2 * LANES + iota((1, LANES), 1),
    )
    all_tiles = rs_v.at[0, pl.ds(0, chips - 1)]
    phase = 5
    pending = []
    for k in range(1, ORDER):
        slot = k - 1
        for i in range(2):
            term(i)
            send_half(
                phase, i, lambda q: part_v.at[term_block(q)], rs_v.at[slot, chip]
            )
        rs_v[slot, chip] = part_v[term_rows, term_cols]
        factor = -(step_size / k)
        wait_bytes(recv_sem, phase, all_tiles)
        new = (factor * mask * summed(slot)).astype(BF16)
        tile_v[slot] = new
        state_v[k, core, term_rows, term_cols] = new
        send_chips(
            phase + 1, lambda q: tile_v.at[slot], state_v.at[(k, core, term_rows, term_cols)]
        )
        wait_bytes(send_sem, phase, all_tiles)
        wait_bytes(recv_sem, phase + 1, all_tiles)
        send(phase + 2, state_v.at[k, core], state_v.at[k, core], partner)
        apply(k, core)
        wait_bytes(recv_sem, phase + 2, state_v.at[k, 0])
        apply(k, 1 - core)
        pending += [(phase + 1, all_tiles), (phase + 2, state_v.at[0, 0])]
        phase += 3

    slot = ORDER - 1
    gather = (iota(square, 1) == gather_row(iota(square, 0))).astype(F32).astype(BF16)
    for i in range(2):
        term(i)
        both = jnp.concatenate(
            [
                jnp.concatenate(
                    [
                        part_v[128 * y : 128 * (y + 1), c * LANES : (c + 1) * LANES]
                        for c in range(2)
                    ],
                    axis=0,
                )
                for y in (2 * i, 2 * i + 1)
            ],
            axis=1,
        )
        both = dot(gather, both).astype(BF16)
        for j in range(2):
            first = 16 * (2 * i + j)
            last_v[first : first + 16] = both[:, j * LANES : (j + 1) * LANES].reshape(
                16, 16, LANES
            )
    send_chips(phase, lambda q: last_v.at[q], rs_v.at[slot, chip])
    rs_v[slot, chip] = last_v[chip]
    own_rows = states // parts
    pick = (iota((8, states), 1) == own_rows * me + iota((8, states), 0)).astype(F32).astype(BF16)
    so_far = []
    for side in range(2):
        total = dot(pick, state_v[0, side])
        for k in range(1, ORDER):
            total += dot(pick, state_v[k, side])
        so_far.append(total)
    wait_bytes(recv_sem, phase, all_tiles)
    total = summed(slot)
    pair_v[0] = total[:8]
    pair_v[1] = total[8:]
    send(phase + 1, pair_v.at[1 - core], pair_v.at[2 + core], partner)
    pair_v[2 + core] = pair_v[core]
    wait_bytes(send_sem, phase + 1, pair_v.at[0])
    wait_bytes(recv_sem, phase + 1, pair_v.at[0])
    for side in range(2):
        from_side = pair_v[2 + side]
        for c in range(2):
            cols = slice(side * half + c * LANES, side * half + (c + 1) * LANES)
            local = slice(c * LANES, (c + 1) * LANES)
            mask = mask_of(
                own_rows * me + iota((own_rows, 1), 0),
                side * half + c * LANES + iota((1, LANES), 1),
            )
            new = -(step_size / ORDER) * mask * from_side[own_rows * c : own_rows * (c + 1)]
            out_ref[:, cols] = so_far[side][:own_rows, local] + new.astype(BF16).astype(F32)

    wait_bytes(send_sem, 0, bw_v.at[0, pl.ds(0, chips - 1)])
    for started in (1, phases - 2):
        wait_bytes(send_sem, started, arrived)
    wait_bytes(send_sem, phases - 1, other_v)
    wait_bytes(send_sem, 2, recv_v.at[pl.ds(0, pairs - group)])
    wait_bytes(send_sem, 3, left_mine)
    wait_bytes(send_sem, 4, bw_v.at[0])
    for started, ref in pending:
        wait_bytes(send_sem, started, ref)
    wait_bytes(send_sem, phase, all_tiles)


def local(site_basis, left_ops, right_ops, integrals, wavefunction, pair_order, sector_sizes):
    states = wavefunction.shape[1]
    pairs = integrals.shape[0]
    per = left_ops.shape[0]
    parts = pairs // per
    vmem = pl.BlockSpec(memory_space=pltpu.VMEM)
    anywhere = pl.BlockSpec(memory_space=pltpu.HBM)
    ops = (2 * per, states, states)
    half = states // 2
    phases = 6 + 3 * ORDER
    body = lambda *refs: kernel(*refs, states=states, pairs=pairs, parts=parts)
    return pl.pallas_call(
        body,
        out_shape=jax.ShapeDtypeStruct(wavefunction.shape, F32),
        in_specs=[anywhere] * 7,
        out_specs=vmem,
        scratch_shapes=[
            pltpu.VMEM((1, pairs), jnp.int32),
            pltpu.SMEM(sector_sizes.shape, jnp.int32),
            pltpu.VMEM(site_basis.shape, BF16),
            pltpu.VMEM(integrals.shape, BF16),
            pltpu.VMEM(wavefunction.shape, BF16),
            pltpu.VMEM(ops, BF16),
            pltpu.VMEM((2, ROWS, LANES), BF16),
            pltpu.VMEM((2, parts // 2, 2, ROWS, LANES), BF16),
            pltpu.VMEM((states, states), BF16),
            pltpu.VMEM(ops, BF16),
            pltpu.VMEM((2 * per, 2, states, half), BF16),
            pltpu.VMEM((pairs, ROWS, LANES), BF16),
            pltpu.VMEM((2, pairs // 2, ROWS * LANES), BF16),
            pltpu.VMEM((pairs, ROWS * LANES), BF16),
            pltpu.VMEM((pairs, ROWS, LANES), BF16),
            pltpu.VMEM((2 * per, half, states), BF16),
            pltpu.VMEM((2, pairs, pairs // 2), BF16),
            pltpu.VMEM((ORDER, 2, states, half), BF16),
            pltpu.VMEM((states, half), BF16),
            pltpu.VMEM((ORDER, parts // 2, ROWS, LANES), BF16),
            pltpu.VMEM((parts // 2, ROWS, LANES), BF16),
            pltpu.VMEM((ORDER, ROWS, LANES), BF16),
            pltpu.VMEM((256, 256), BF16),
            pltpu.VMEM((4, 8, LANES), F32),
            pltpu.VMEM((per, half, states), BF16),
            pltpu.VMEM((pairs, ROWS * LANES), F32),
            pltpu.SemaphoreType.DMA((7,)),
            pltpu.SemaphoreType.DMA((phases,)),
            pltpu.SemaphoreType.DMA((phases,)),
        ],
        compiler_params=pltpu.CompilerParams(
            collective_id=0, has_side_effects=True, vmem_limit_bytes=62 << 20
        ),
    )(
        pair_order.reshape(1, pairs), sector_sizes, site_basis, left_ops, right_ops,
        integrals, wavefunction,
    )


def solution(mesh):
    in_specs = (
        P(BOTH, None), P(BOTH, None, None), P(BOTH, None, None), P(), P(BOTH, None), P(), P()
    )
    return jax.shard_map(
        local, mesh=mesh, in_specs=in_specs, out_specs=P(BOTH, None), check_vma=False
    )
```

```python
import math

import jax
import jax.numpy as jnp
from jax import lax
from jax.experimental import pallas as pl
from jax.experimental.pallas import tpu as pltpu
from jax.sharding import PartitionSpec as P

ORDER = 3
ROWS, LANES = 16, 128
BF16, F32 = jnp.bfloat16, jnp.float32
BOTH = ("wide", "narrow")
MESH = pl.DeviceIdType.MESH


def dot(a, b, dims=((1,), (0,))):
    return lax.dot_general(a, b, (dims, ((), ())), preferred_element_type=F32)


def iota(shape, dim):
    return lax.broadcasted_iota(jnp.int32, shape, dim)


def tile_swap(size):
    o, m = iota((size, size), 0), iota((size, size), 1)
    return (m == (o & 15) * 16 + (o >> 4)).astype(F32).astype(BF16)


def spread_row(o):
    return ((o & 63) >> 2) * 16 + (o >> 6) * 4 + (o & 3)


def gather_row(o):
    return ((o >> 2) & 1) * 128 + ((o >> 3) & 1) * 64 + (o >> 4) * 4 + (o & 3)


def far_first(depth):
    steps = [
        (dy, dx, dz) for dy in range(4) for dx in range(4) for dz in range(depth)
    ]
    hops = lambda d: min(d[0], 4 - d[0]) + min(d[1], 4 - d[1])
    along_z = lambda d: min(d[2], 4 - d[2]) if depth == 4 else 2 * d[2]
    return sorted(steps, key=lambda d: -hops(d) - along_z(d))


def kernel(
    order_ref, sizes_ref, basis_ref, left_ref, right_ref, integrals_ref, wave_ref,
    out_ref,
    order_v, sizes_v, basis_v, integrals_v, wave_v,
    left_v, pack_v, basis_all, wave_all, u_v, built_v, applied_v, recv_v, bm_v, ym_v, cbuf_v, comp_v,
    mix_v, state_v, part_v, rs_v, last_v, tile_v, swap_v, pair_v, other_v, acc_v, meet_v, met_v, local_sem, send_sem, recv_sem,
    *, states, pairs, parts,
):
    per = pairs // parts
    phases = 8 + 3 * ORDER
    group = 2 * per
    narrow = lax.axis_size("narrow")
    w, n = lax.axis_index("wide"), lax.axis_index("narrow")
    core = lax.rem(w, 2)
    me = w * narrow + n
    chips = parts // 2
    chip = w // 2 * narrow + n
    partner = (w + 1 - 2 * core, n)
    across = states // LANES
    half = states // 2
    step_size = 2.0 / math.sqrt(pairs)

    y, x, z = w // 2, n // 4, lax.rem(n, 4)

    to_w = [lax.rem(y + d, 4) * 2 + core for d in range(4)]
    to_y = [lax.rem(y + d, 4) * narrow for d in range(4)]
    to_x = [lax.rem(x + d, 4) * 4 for d in range(4)]
    to_z = [lax.rem(z + d, 4) for d in range(4)]

    def block(row, col):
        return (
            pl.ds(pl.multiple_of(row * ROWS, ROWS), ROWS),
            pl.ds(pl.multiple_of(col * LANES, LANES), LANES),
        )

    def mix_block(q):
        return block(lax.div(q, across), lax.rem(q, across))

    def term_block(q):
        return block(lax.rem(q, 2) * (chips // 4) + lax.div(q, 4), lax.div(lax.rem(q, 4), 2))

    def mix_slots(q):
        return pl.ds((lax.rem(q, 2) * (chips // 2) + lax.div(q, 2)) * group, group)

    def send(phase, src, dst, device):
        pltpu.make_async_remote_copy(
            src_ref=src, dst_ref=dst, send_sem=send_sem.at[phase],
            recv_sem=recv_sem.at[phase], device_id=device, device_id_type=MESH,
        ).start()

    def each_chip(visit):
        to_n = [[i + j for j in to_z] for i in to_x]
        for dy, dx, dz in far_first(4):
            if (dy, dx, dz) != (0, 0, 0):
                visit(to_y[dy] + to_n[dx][dz], (to_w[dy], to_n[dx][dz]))

    def send_chips(phase, src, dst):
        each_chip(lambda q, device: send(phase, src(q), dst, device))

    def send_half(phase, parity, src, dst):
        first = lax.rem(parity + z, 2)
        to_n = [[i + lax.rem(z + first + 2 * j, 4) for j in range(2)] for i in to_x]
        for dy, dx, dz in far_first(2):
            q, device = to_y[dy] + to_n[dx][dz], (to_w[dy], to_n[dx][dz])
            if (dy, dx, dz) == (0, 0, 0):

                @pl.when(first == 1)
                def _():
                    send(phase, src(q), dst, device)

            else:
                send(phase, src(q), dst, device)

    def wait_bytes(sem, phase, ref):
        pltpu.make_async_copy(ref, ref, sem.at[phase]).wait()

    barrier = pltpu.get_barrier_semaphore()

    def greet(device):
        pl.semaphore_signal(barrier, inc=1, device_id=device, device_id_type=MESH)

    greet(partner)
    each_chip(lambda q, device: greet(device))
    half_rows = half // ROWS
    own_half = pl.ds(pl.multiple_of(core * half, half), half)
    other_half = pl.ds(pl.multiple_of((1 - core) * half, half), half)
    own_slots = pl.ds(core * (pairs // 2) + chip * per, per)
    other_slots = pl.ds((1 - core) * (pairs // 2) + chip * per, per)
    mix_rows, mix_cols = mix_block(chip)
    term_rows, term_cols = term_block(chip)
    loads = [
        pltpu.make_async_copy(src, dst, local_sem.at[i])
        for i, (src, dst) in enumerate(
            [
                (order_ref, order_v), (sizes_ref, sizes_v), (integrals_ref, integrals_v),
                (basis_ref, basis_v), (wave_ref, wave_v),
                (right_ref.at[:, block(core * half_rows + chip // across, 0)[0], mix_cols],
                 recv_v.at[own_slots]),
                (left_ref, left_v.at[pl.ds(core * per, per)]),
            ]
        )
    ]
    for load in loads:
        load.start()
    for load in loads[:5]:
        load.wait()

    def packed(ref):
        rows = ref[...].astype(F32)
        return jnp.concatenate(
            [rows[:, c * LANES : (c + 1) * LANES] for c in range(across)], axis=0
        ).astype(BF16)

    pack_v[0] = packed(basis_v)
    pack_v[1] = packed(wave_v)
    by_z = z * (chips // 4) + y * 4 + x
    basis_all[core, chip] = pack_v[0]
    wave_all[core, by_z] = pack_v[1]
    swap_v[...] = tile_swap(256)

    def take(ids, width):
        return (iota((pairs, width), 0) == ids).astype(F32).astype(BF16)

    def slot(of_chip, of_core, j):
        return ((of_chip // narrow * 2 + of_core) * narrow + (of_chip & (narrow - 1))) * per + j

    chosen = take(order_v[...], pairs)
    place = iota((1, pairs), 1)
    owner = (place * (65536 // group + 1)) >> 16
    rest = place - owner * group
    of_core = (rest >= per).astype(jnp.int32)
    owner = (owner & (chips // 2 - 1)) * 2 + owner // (chips // 2)
    by_row = dot(chosen, take(slot(owner, of_core, rest - of_core * per), pairs)).astype(BF16)
    place = iota((1, pairs // 2), 1)
    sender = (place * (65536 // per + 1)) >> 16
    for c in range(2):
        by_column = dot(chosen, take(slot(sender, c, place - sender * per), pairs // 2))
        by_column = dot(integrals_v[...], by_column.astype(BF16)).astype(BF16)
        mix_v[c] = dot(by_row, by_column, ((0,), (0,))).astype(BF16)

    ends, total = [], jnp.int32(0)
    for b in range(sizes_ref.shape[0]):
        total = total + sizes_v[b]
        ends.append(total)

    def block_of(ids):
        found = jnp.zeros_like(ids)
        for end in ends:
            found = found + (ids >= end).astype(jnp.int32)
        return found

    def mask_of(row_ids, col_ids):
        return (jnp.abs(block_of(row_ids) - block_of(col_ids)) <= 2).astype(F32)

    pl.semaphore_wait(barrier, chips)

    send(phases - 1, right_ref.at[:, other_half, :], other_v, partner)
    for a in (2, 1, 3, 0):
        for b in (2, 1, 3, 0):
            if (a, b) != (0, 0):
                send(0, pack_v.at[0], basis_all.at[core, chip], (w, to_x[a] + to_z[b]))
                send(0, pack_v.at[1], wave_all.at[core, by_z], (to_w[a], to_x[b] + z))
    send_chips(
        1,
        lambda q: right_ref.at[
            (slice(None), *block(core * half_rows + lax.div(q, across), lax.rem(q, across)))
        ],
        recv_v.at[own_slots],
    )
    wait_bytes(recv_sem, phases - 1, other_v)
    send_chips(phases - 2, lambda q: other_v.at[(slice(None), *mix_block(q))], recv_v.at[other_slots])
    recv_v[other_slots] = other_v[:, mix_rows, mix_cols]
    plane = chips // 4
    wait_bytes(recv_sem, 0, basis_all.at[0, pl.ds(0, 2 * plane - 2)])
    for d in (2, 1, 3):
        block_of_y = basis_all.at[core, pl.ds(y * plane, plane)]
        send(4, block_of_y, block_of_y, (to_w[d], n))
        block_of_z = wave_all.at[core, pl.ds(z * plane, plane)]
        send(4, block_of_z, block_of_z, (w, to_x[0] + to_z[d]))
    left_mine = left_v.at[pl.ds(core * per, per)]
    send(3, left_ref, left_mine, partner)

    def into_rows(c):
        def some(q, carry):
            base = pl.multiple_of(q * 32, 32)
            both = jnp.concatenate(
                [
                    recv_v[pl.ds(c * (pairs // 2) + base + 16 * i, 16)].reshape(256, LANES)
                    for i in range(2)
                ],
                axis=1,
            )
            both = dot(swap_v[...], both).astype(BF16)
            for r in range(16):
                for i in range(2):
                    bm_v[c, pl.ds(base + 16 * i, 16), r * LANES : (r + 1) * LANES] = both[
                        16 * r : 16 * (r + 1), i * LANES : (i + 1) * LANES
                    ]
            return carry

        lax.fori_loop(0, pairs // 64, some, 0, unroll=True)

    def col_chunk(j):
        return pl.ds(pl.multiple_of(j * 256, 256), 256)

    arrived = recv_v.at[pl.ds(0, (chips - 1) * per)]
    loads[5].wait()
    wait_bytes(recv_sem, 1, arrived)
    into_rows(core)

    def mix_first(j, carry):
        acc_v[:, col_chunk(j)] = dot(mix_v[core], bm_v[core, :, col_chunk(j)])
        return carry

    lax.fori_loop(0, 8, mix_first, 0, unroll=True)
    wait_bytes(recv_sem, phases - 2, arrived)
    into_rows(1 - core)
    for i in range(2):
        rows = slice(i * (pairs // 2), (i + 1) * (pairs // 2))

        def mix_second(j, carry, rows=rows):
            ym_v[rows, col_chunk(j)] = (
                acc_v[rows, col_chunk(j)]
                + dot(mix_v[1 - core, rows, :], bm_v[1 - core, :, col_chunk(j)])
            ).astype(BF16)
            return carry

        lax.fori_loop(0, 8, mix_second, 0, unroll=True)

        def into_tiles(q, carry, i=i):
            base = pl.multiple_of(q * 32 + i * (pairs // 2), 32)
            both = jnp.concatenate(
                [
                    jnp.concatenate(
                        [
                            ym_v[pl.ds(base + 16 * j, 16), r * LANES : (r + 1) * LANES]
                            for r in range(16)
                        ],
                        axis=0,
                    )
                    for j in range(2)
                ],
                axis=1,
            )
            both = dot(swap_v[...], both).astype(BF16)
            for j in range(2):
                cbuf_v[pl.ds(base + 16 * j, 16)] = both[
                    :, j * LANES : (j + 1) * LANES
                ].reshape(16, 16, LANES)
            return carry

        lax.fori_loop(0, pairs // 64, into_tiles, 0, unroll=True)
        send_half(
            2, i, lambda q: cbuf_v.at[mix_slots(q)], comp_v.at[:, mix_rows, mix_cols]
        )
    comp_v[:, mix_rows, mix_cols] = cbuf_v[mix_slots(chip)]

    wait_bytes(recv_sem, 4, recv_v.at[pl.ds(0, 6 * plane)])
    send(phases - 3, basis_all.at[core], basis_all.at[core], partner)
    send(phases - 4, wave_all.at[core], wave_all.at[core], partner)
    wait_bytes(recv_sem, phases - 3, basis_all.at[0])
    wait_bytes(recv_sem, phases - 4, wave_all.at[0])
    square = (256, 256)
    spread = (iota(square, 1) == spread_row(iota(square, 0))).astype(F32).astype(BF16)
    for g in range(states // 64):
        waves = [
            wave_all[g % 2, (i % 4) * plane + g // 2 * 4 + i // 4] for i in range(plane)
        ]
        both = jnp.concatenate(
            [
                basis_all[g % 2, g // 2 * plane : (g // 2 + 1) * plane].reshape(256, LANES),
                jnp.concatenate(waves, axis=0),
            ],
            axis=1,
        )
        both = dot(spread, both)
        for c in range(across):
            rows, cols = slice(64 * g, 64 * (g + 1)), slice(c * LANES, (c + 1) * LANES)
            mask = mask_of(
                64 * g + iota((64, 1), 0), c * LANES + iota((1, LANES), 1)
            )
            tile = both[64 * c : 64 * (c + 1)]
            u_v[rows, cols] = tile[:, :LANES].astype(BF16)
            state_v[0, c // 2, rows, c % 2 * LANES : (c % 2 + 1) * LANES] = (
                tile[:, LANES:] * mask
            ).astype(BF16)

    loads[6].wait()
    wait_bytes(recv_sem, 3, left_mine)

    def build(s, carry):
        rotated = dot(left_v[s], u_v[...]).astype(BF16)
        built_v[s] = dot(u_v[...], rotated, ((0,), (0,))).astype(BF16)
        return carry

    lax.fori_loop(0, group, build, 0)

    def apply(s, carry):
        for side in range(2):
            applied_v[s, side] = dot(built_v[s], state_v[0, side]).astype(BF16)
        return carry

    lax.fori_loop(0, group, apply, 0)
    wait_bytes(recv_sem, 2, cbuf_v.at[pl.ds(0, pairs - group)])

    def mine_of(side):
        return pl.ds(pl.multiple_of(side * half, half), half)

    def meet_own(k):
        def one(s, carry):
            meet_v[s] = dot(state_v[k, core], comp_v[s, :, mine_of(core)], ((1,), (1,)))
            return carry

        lax.fori_loop(0, group, one, 0, unroll=True)

    def meet_other(k):
        def one(s, carry):
            met_v[s] = (
                meet_v[s]
                + dot(state_v[k, 1 - core], comp_v[s, :, mine_of(1 - core)], ((1,), (1,)))
            ).astype(BF16)
            return carry

        lax.fori_loop(0, group, one, 0, unroll=True)

    def later_term(i):
        rows = slice(i * half, (i + 1) * half)
        total = dot(built_v[0, rows, :], met_v[0])
        for s in range(1, group):
            total += dot(built_v[s, rows, :], met_v[s])
        part_v[rows, :] = total.astype(BF16)

    def first_term(i):
        rows = slice(i * half, (i + 1) * half)
        total = jnp.zeros((half, half), F32)
        for s in range(group):
            for side in range(2):
                total += dot(
                    applied_v[s, side, rows, :],
                    comp_v[s, :, side * half : (side + 1) * half],
                    ((1,), (1,)),
                )
        part_v[rows, :] = total.astype(BF16)

    def summed(slot):
        def some(j, carry):
            return carry + jnp.sum(rs_v[slot, pl.ds(j * 8, 8)].astype(F32), axis=0)

        return lax.fori_loop(0, chips // 8, some, jnp.zeros((ROWS, LANES), F32), unroll=True)

    mask = mask_of(
        lax.rem(chip, 2) * half + chip // 4 * ROWS + iota((ROWS, 1), 0),
        core * half + lax.rem(chip, 4) // 2 * LANES + iota((1, LANES), 1),
    )
    all_tiles = rs_v.at[0, pl.ds(0, chips - 1)]
    phase = 5
    pending = []
    for k in range(1, ORDER):
        slot = k - 1
        for i in range(2):
            first_term(i) if k == 1 else later_term(i)
            send_half(
                phase, i, lambda q: part_v.at[term_block(q)], rs_v.at[slot, chip]
            )
        rs_v[slot, chip] = part_v[term_rows, term_cols]
        factor = -(step_size / k)
        wait_bytes(recv_sem, phase, all_tiles)
        new = (factor * mask * summed(slot)).astype(BF16)
        tile_v[slot] = new
        state_v[k, core, term_rows, term_cols] = new
        send_chips(
            phase + 1, lambda q: tile_v.at[slot], state_v.at[(k, core, term_rows, term_cols)]
        )
        wait_bytes(send_sem, phase, all_tiles)
        wait_bytes(recv_sem, phase + 1, all_tiles)
        send(phase + 2, state_v.at[k, core], state_v.at[k, core], partner)
        meet_own(k)
        wait_bytes(recv_sem, phase + 2, state_v.at[k, 0])
        meet_other(k)
        pending += [(phase + 1, all_tiles), (phase + 2, state_v.at[0, 0])]
        phase += 3

    slot = ORDER - 1
    gather = (iota(square, 1) == gather_row(iota(square, 0))).astype(F32).astype(BF16)
    for i in range(2):
        later_term(i)
        both = jnp.concatenate(
            [
                jnp.concatenate(
                    [
                        part_v[128 * y : 128 * (y + 1), c * LANES : (c + 1) * LANES]
                        for c in range(2)
                    ],
                    axis=0,
                )
                for y in (2 * i, 2 * i + 1)
            ],
            axis=1,
        )
        both = dot(gather, both).astype(BF16)
        for j in range(2):
            first = 16 * (2 * i + j)
            last_v[first : first + 16] = both[:, j * LANES : (j + 1) * LANES].reshape(
                16, 16, LANES
            )
        for j in (2 * i, 2 * i + 1):
            for a in (2, 1, 3, 0):
                for b in (2, 1, 3, 0):
                    to_n = to_x[a] + to_z[b]
                    device = (2 * j + core, to_n)
                    from_tile = last_v.at[j * narrow + to_n]
                    if (a, b) == (0, 0):

                        @pl.when(y != j)
                        def _():
                            send(phase, from_tile, rs_v.at[slot, chip], device)

                    else:
                        send(phase, from_tile, rs_v.at[slot, chip], device)
    rs_v[slot, chip] = last_v[chip]
    own_rows = states // parts
    pick = (iota((8, states), 1) == own_rows * me + iota((8, states), 0)).astype(F32).astype(BF16)
    so_far = []
    for side in range(2):
        total = dot(pick, state_v[0, side])
        for k in range(1, ORDER):
            total += dot(pick, state_v[k, side])
        so_far.append(total)
    wait_bytes(recv_sem, phase, all_tiles)
    total = summed(slot)
    pair_v[0] = total[:8]
    pair_v[1] = total[8:]
    send(phase + 1, pair_v.at[1 - core], pair_v.at[2 + core], partner)
    pair_v[2 + core] = pair_v[core]
    wait_bytes(send_sem, phase + 1, pair_v.at[0])
    wait_bytes(recv_sem, phase + 1, pair_v.at[0])
    for side in range(2):
        from_side = pair_v[2 + side]
        for c in range(2):
            cols = slice(side * half + c * LANES, side * half + (c + 1) * LANES)
            local = slice(c * LANES, (c + 1) * LANES)
            mask = mask_of(
                own_rows * me + iota((own_rows, 1), 0),
                side * half + c * LANES + iota((1, LANES), 1),
            )
            new = -(step_size / ORDER) * mask * from_side[own_rows * c : own_rows * (c + 1)]
            out_ref[:, cols] = so_far[side][:own_rows, local] + new.astype(BF16).astype(F32)

    wait_bytes(send_sem, 0, basis_all.at[0, pl.ds(0, 2 * plane - 2)])
    for started in (1, phases - 2):
        wait_bytes(send_sem, started, arrived)
    wait_bytes(send_sem, phases - 1, other_v)
    wait_bytes(send_sem, 2, recv_v.at[pl.ds(0, pairs - group)])
    wait_bytes(send_sem, 3, left_mine)
    wait_bytes(send_sem, 4, recv_v.at[pl.ds(0, 6 * plane)])
    wait_bytes(send_sem, phases - 3, basis_all.at[0])
    wait_bytes(send_sem, phases - 4, wave_all.at[0])
    for started, ref in pending:
        wait_bytes(send_sem, started, ref)
    wait_bytes(send_sem, phase, all_tiles)


def local(site_basis, left_ops, right_ops, integrals, wavefunction, pair_order, sector_sizes):
    states = wavefunction.shape[1]
    pairs = integrals.shape[0]
    per = left_ops.shape[0]
    parts = pairs // per
    vmem = pl.BlockSpec(memory_space=pltpu.VMEM)
    anywhere = pl.BlockSpec(memory_space=pltpu.HBM)
    ops = (2 * per, states, states)
    half = states // 2
    phases = 8 + 3 * ORDER
    body = lambda *refs: kernel(*refs, states=states, pairs=pairs, parts=parts)
    return pl.pallas_call(
        body,
        out_shape=jax.ShapeDtypeStruct(wavefunction.shape, F32),
        in_specs=[anywhere] * 7,
        out_specs=vmem,
        scratch_shapes=[
            pltpu.VMEM((1, pairs), jnp.int32),
            pltpu.SMEM(sector_sizes.shape, jnp.int32),
            pltpu.VMEM(site_basis.shape, BF16),
            pltpu.VMEM(integrals.shape, BF16),
            pltpu.VMEM(wavefunction.shape, BF16),
            pltpu.VMEM(ops, BF16),
            pltpu.VMEM((2, ROWS, LANES), BF16),
            pltpu.VMEM((2, parts // 2, ROWS, LANES), BF16),
            pltpu.VMEM((2, parts // 2, ROWS, LANES), BF16),
            pltpu.VMEM((states, states), BF16),
            pltpu.VMEM(ops, BF16),
            pltpu.VMEM((2 * per, 2, states, half), BF16),
            pltpu.VMEM((pairs, ROWS, LANES), BF16),
            pltpu.VMEM((2, pairs // 2, ROWS * LANES), BF16),
            pltpu.VMEM((pairs, ROWS * LANES), BF16),
            pltpu.VMEM((pairs, ROWS, LANES), BF16),
            pltpu.VMEM((2 * per, half, states), BF16),
            pltpu.VMEM((2, pairs, pairs // 2), BF16),
            pltpu.VMEM((ORDER, 2, states, half), BF16),
            pltpu.VMEM((states, half), BF16),
            pltpu.VMEM((ORDER, parts // 2, ROWS, LANES), BF16),
            pltpu.VMEM((parts // 2, ROWS, LANES), BF16),
            pltpu.VMEM((ORDER, ROWS, LANES), BF16),
            pltpu.VMEM((256, 256), BF16),
            pltpu.VMEM((4, 8, LANES), F32),
            pltpu.VMEM((per, half, states), BF16),
            pltpu.VMEM((pairs, ROWS * LANES), F32),
            pltpu.VMEM((2 * per, states, half), F32),
            pltpu.VMEM((2 * per, states, half), BF16),
            pltpu.SemaphoreType.DMA((7,)),
            pltpu.SemaphoreType.DMA((phases,)),
            pltpu.SemaphoreType.DMA((phases,)),
        ],
        compiler_params=pltpu.CompilerParams(
            collective_id=0, has_side_effects=True, vmem_limit_bytes=62 << 20
        ),
    )(
        pair_order.reshape(1, pairs), sector_sizes, site_basis, left_ops, right_ops,
        integrals, wavefunction,
    )


def solution(mesh):
    in_specs = (
        P(BOTH, None), P(BOTH, None, None), P(BOTH, None, None), P(), P(BOTH, None), P(), P()
    )
    return jax.shard_map(
        local, mesh=mesh, in_specs=in_specs, out_specs=P(BOTH, None), check_vma=False
    )
```

```python
import math

import jax
import jax.numpy as jnp
from jax import lax
from jax.experimental import pallas as pl
from jax.experimental.pallas import tpu as pltpu
from jax.sharding import PartitionSpec as P

ORDER = 3
ROWS, LANES = 16, 128
BF16, F32 = jnp.bfloat16, jnp.float32
BOTH = ("wide", "narrow")
MESH = pl.DeviceIdType.MESH


def dot(a, b, dims=((1,), (0,))):
    return lax.dot_general(a, b, (dims, ((), ())), preferred_element_type=F32)


def iota(shape, dim):
    return lax.broadcasted_iota(jnp.int32, shape, dim)


def tile_swap(size):
    o, m = iota((size, size), 0), iota((size, size), 1)
    return (m == (o & 15) * 16 + (o >> 4)).astype(F32).astype(BF16)


def spread_row(o):
    return ((o & 63) >> 2) * 16 + (o >> 6) * 4 + (o & 3)


def gather_row(o):
    return ((o >> 2) & 1) * 128 + ((o >> 3) & 1) * 64 + (o >> 4) * 4 + (o & 3)


def far_first(depth):
    steps = [
        (dy, dx, dz) for dy in range(4) for dx in range(4) for dz in range(depth)
    ]
    hops = lambda d: min(d[0], 4 - d[0]) + min(d[1], 4 - d[1])
    along_z = lambda d: min(d[2], 4 - d[2]) if depth == 4 else 2 * d[2]
    return sorted(steps, key=lambda d: -hops(d) - along_z(d))


def kernel(
    order_ref, sizes_ref, basis_ref, left_ref, right_ref, integrals_ref, wave_ref,
    out_ref,
    order_v, sizes_v, basis_v, integrals_v, wave_v,
    left_v, pack_v, basis_all, wave_all, u_v, built_v, applied_v, recv_v, bm_v, ym_v, cbuf_v, comp_v,
    mix_v, state_v, part_v, rs_v, last_v, tile_v, swap_v, pair_v, other_v, acc_v, meet_v, met_v, local_sem, send_sem, recv_sem,
    *, states, pairs, parts,
):
    per = pairs // parts
    phases = 8 + 3 * ORDER
    group = 2 * per
    narrow = lax.axis_size("narrow")
    w, n = lax.axis_index("wide"), lax.axis_index("narrow")
    core = lax.rem(w, 2)
    me = w * narrow + n
    chips = parts // 2
    chip = w // 2 * narrow + n
    partner = (w + 1 - 2 * core, n)
    across = states // LANES
    half = states // 2
    step_size = 2.0 / math.sqrt(pairs)

    y, x, z = w // 2, n // 4, lax.rem(n, 4)

    to_w = [lax.rem(y + d, 4) * 2 + core for d in range(4)]
    to_y = [lax.rem(y + d, 4) * narrow for d in range(4)]
    to_x = [lax.rem(x + d, 4) * 4 for d in range(4)]
    to_z = [lax.rem(z + d, 4) for d in range(4)]

    def block(row, col):
        return (
            pl.ds(pl.multiple_of(row * ROWS, ROWS), ROWS),
            pl.ds(pl.multiple_of(col * LANES, LANES), LANES),
        )

    def mix_block(q):
        return block(lax.div(q, across), lax.rem(q, across))

    def term_block(q):
        return block(lax.rem(q, 2) * (chips // 4) + lax.div(q, 4), lax.div(lax.rem(q, 4), 2))

    def send(phase, src, dst, device):
        pltpu.make_async_remote_copy(
            src_ref=src, dst_ref=dst, send_sem=send_sem.at[phase],
            recv_sem=recv_sem.at[phase], device_id=device, device_id_type=MESH,
        ).start()

    to_n = [[i + j for j in to_z] for i in to_x]
    reached = [
        (to_y[dy] + to_n[dx][dz], (to_w[dy], to_n[dx][dz])) for dy, dx, dz in far_first(4)
    ]

    def each_chip(visit):
        for q, device in reached[:-1]:
            visit(q, device)

    def send_chips(phase, src, dst):
        each_chip(lambda q, device: send(phase, src(q), dst, device))

    turn = lax.rem(x + y + z, 2)

    def send_half(phase, parity, dst):
        first = lax.rem(parity + z, 2)
        at_z = [lax.rem(z + first + 2 * j, 4) for j in range(2)]
        half_z = [lax.div(j, 2) for j in at_z]
        at_yx = [[lax.div(i + j, 4) for j in to_x] for i in to_y]
        for dy, dx, dz in far_first(2):
            src = part_v.at[parity, half_z[dz], at_yx[dy][dx]]
            device = (to_w[dy], to_x[dx] + at_z[dz])
            if (dy, dx, dz) == (0, 0, 0):

                @pl.when(first == 1)
                def _():
                    send(phase, src, dst, device)

            else:
                send(phase, src, dst, device)

    def wait_bytes(sem, phase, ref):
        pltpu.make_async_copy(ref, ref, sem.at[phase]).wait()

    barrier = pltpu.get_barrier_semaphore()

    def greet(device):
        pl.semaphore_signal(barrier, inc=1, device_id=device, device_id_type=MESH)

    greet(partner)
    each_chip(lambda q, device: greet(device))
    half_rows = half // ROWS
    own_half = pl.ds(pl.multiple_of(core * half, half), half)
    other_half = pl.ds(pl.multiple_of((1 - core) * half, half), half)
    own_slots = pl.ds(core * (pairs // 2) + chip * per, per)
    other_slots = pl.ds((1 - core) * (pairs // 2) + chip * per, per)
    mix_rows, mix_cols = mix_block(chip)
    term_rows, term_cols = term_block(chip)
    loads = [
        pltpu.make_async_copy(src, dst, local_sem.at[i])
        for i, (src, dst) in enumerate(
            [
                (order_ref, order_v), (sizes_ref, sizes_v), (integrals_ref, integrals_v),
                (basis_ref, basis_v), (wave_ref, wave_v),
                (right_ref.at[:, block(core * half_rows + chip // across, 0)[0], mix_cols],
                 recv_v.at[own_slots]),
                (left_ref, left_v.at[pl.ds(core * per, per)]),
            ]
        )
    ]
    for load in loads:
        load.start()
    for load in loads[:5]:
        load.wait()

    def packed(ref):
        rows = ref[...].astype(F32)
        return jnp.concatenate(
            [rows[:, c * LANES : (c + 1) * LANES] for c in range(across)], axis=0
        ).astype(BF16)

    pack_v[0] = packed(basis_v)
    pack_v[1] = packed(wave_v)
    by_z = z * (chips // 4) + y * 4 + x
    basis_all[core, chip] = pack_v[0]
    wave_all[core, by_z] = pack_v[1]
    swap_v[...] = tile_swap(256)

    def take(ids, width):
        return (iota((pairs, width), 0) == ids).astype(F32).astype(BF16)

    def slot(of_chip, of_core, j):
        return ((of_chip // narrow * 2 + of_core) * narrow + (of_chip & (narrow - 1))) * per + j

    chosen = take(order_v[...], pairs)
    place = iota((1, pairs), 1)
    owner = (place * (65536 // group + 1)) >> 16
    rest = place - owner * group
    of_core = (rest >= per).astype(jnp.int32)
    order_of_owners = owner
    for i, (q, _) in enumerate(reached):
        owner = jnp.where(order_of_owners == i, q, owner)
    by_row = dot(chosen, take(slot(owner, of_core, rest - of_core * per), pairs)).astype(BF16)
    place = iota((1, pairs // 2), 1)
    sender = (place * (65536 // per + 1)) >> 16
    for c in range(2):
        by_column = dot(chosen, take(slot(sender, c, place - sender * per), pairs // 2))
        by_column = dot(integrals_v[...], by_column.astype(BF16)).astype(BF16)
        mix_v[c] = dot(by_row, by_column, ((0,), (0,))).astype(BF16)

    ends, total = [], jnp.int32(0)
    for b in range(sizes_ref.shape[0]):
        total = total + sizes_v[b]
        ends.append(total)

    def block_of(ids):
        found = jnp.zeros_like(ids)
        for end in ends:
            found = found + (ids >= end).astype(jnp.int32)
        return found

    def mask_of(row_ids, col_ids):
        return (jnp.abs(block_of(row_ids) - block_of(col_ids)) <= 2).astype(F32)

    pl.semaphore_wait(barrier, chips)

    send(phases - 1, right_ref.at[:, other_half, :], other_v, partner)
    for a in (2, 1, 3, 0):
        for b in (2, 1, 3, 0):
            if (a, b) != (0, 0):
                send(0, pack_v.at[0], basis_all.at[core, chip], (w, to_x[a] + to_z[b]))
                send(0, pack_v.at[1], wave_all.at[core, by_z], (to_w[a], to_x[b] + z))
    send_chips(
        1,
        lambda q: right_ref.at[
            (slice(None), *block(core * half_rows + lax.div(q, across), lax.rem(q, across)))
        ],
        recv_v.at[own_slots],
    )
    wait_bytes(recv_sem, phases - 1, other_v)
    send_chips(phases - 2, lambda q: other_v.at[(slice(None), *mix_block(q))], recv_v.at[other_slots])
    recv_v[other_slots] = other_v[:, mix_rows, mix_cols]
    plane = chips // 4
    wait_bytes(recv_sem, 0, basis_all.at[0, pl.ds(0, 2 * plane - 2)])
    for d in (2, 1, 3):
        block_of_y = basis_all.at[core, pl.ds(y * plane, plane)]
        send(4, block_of_y, block_of_y, (to_w[d], n))
        block_of_z = wave_all.at[core, pl.ds(z * plane, plane)]
        send(4, block_of_z, block_of_z, (w, to_x[0] + to_z[d]))
    left_mine = left_v.at[pl.ds(core * per, per)]
    send(3, left_ref, left_mine, partner)

    def into_rows(c):
        def some(q, carry):
            base = pl.multiple_of(q * 32, 32)
            both = jnp.concatenate(
                [
                    recv_v[pl.ds(c * (pairs // 2) + base + 16 * i, 16)].reshape(256, LANES)
                    for i in range(2)
                ],
                axis=1,
            )
            both = dot(swap_v[...], both).astype(BF16)
            for r in range(16):
                for i in range(2):
                    bm_v[c, pl.ds(base + 16 * i, 16), r * LANES : (r + 1) * LANES] = both[
                        16 * r : 16 * (r + 1), i * LANES : (i + 1) * LANES
                    ]
            return carry

        lax.fori_loop(0, pairs // 64, some, 0, unroll=True)

    def col_chunk(j):
        return pl.ds(pl.multiple_of(j * 256, 256), 256)

    arrived = recv_v.at[pl.ds(0, (chips - 1) * per)]
    loads[5].wait()
    wait_bytes(recv_sem, 1, arrived)
    into_rows(core)

    def mix_first(j, carry):
        acc_v[:, col_chunk(j)] = dot(mix_v[core], bm_v[core, :, col_chunk(j)])
        return carry

    lax.fori_loop(0, 8, mix_first, 0, unroll=True)
    wait_bytes(recv_sem, phases - 2, arrived)
    into_rows(1 - core)
    for i in range(2):
        rows = slice(i * (pairs // 2), (i + 1) * (pairs // 2))

        def mix_second(j, carry, rows=rows):
            ym_v[rows, col_chunk(j)] = (
                acc_v[rows, col_chunk(j)]
                + dot(mix_v[1 - core, rows, :], bm_v[1 - core, :, col_chunk(j)])
            ).astype(BF16)
            return carry

        lax.fori_loop(0, 8, mix_second, 0, unroll=True)

        def into_tiles(q, carry, i=i):
            base = pl.multiple_of(q * 32 + i * (pairs // 2), 32)
            both = jnp.concatenate(
                [
                    jnp.concatenate(
                        [
                            ym_v[pl.ds(base + 16 * j, 16), r * LANES : (r + 1) * LANES]
                            for r in range(16)
                        ],
                        axis=0,
                    )
                    for j in range(2)
                ],
                axis=1,
            )
            both = dot(swap_v[...], both).astype(BF16)
            for j in range(2):
                cbuf_v[pl.ds(base + 16 * j, 16)] = both[
                    :, j * LANES : (j + 1) * LANES
                ].reshape(16, 16, LANES)
            return carry

        lax.fori_loop(0, pairs // 64, into_tiles, 0, unroll=True)
        for j in range(i * (chips // 2), min((i + 1) * (chips // 2), chips - 1)):
            send(
                2,
                cbuf_v.at[pl.ds(j * group, group)],
                comp_v.at[:, mix_rows, mix_cols],
                reached[j][1],
            )
    comp_v[:, mix_rows, mix_cols] = cbuf_v[pairs - group :]

    wait_bytes(recv_sem, 4, recv_v.at[pl.ds(0, 6 * plane)])
    send(phases - 3, basis_all.at[core], basis_all.at[core], partner)
    send(phases - 4, wave_all.at[core], wave_all.at[core], partner)
    wait_bytes(recv_sem, phases - 3, basis_all.at[0])
    wait_bytes(recv_sem, phases - 4, wave_all.at[0])
    square = (256, 256)
    spread = (iota(square, 1) == spread_row(iota(square, 0))).astype(F32).astype(BF16)
    for g in range(states // 64):
        waves = [
            wave_all[g % 2, (i % 4) * plane + g // 2 * 4 + i // 4] for i in range(plane)
        ]
        both = jnp.concatenate(
            [
                basis_all[g % 2, g // 2 * plane : (g // 2 + 1) * plane].reshape(256, LANES),
                jnp.concatenate(waves, axis=0),
            ],
            axis=1,
        )
        both = dot(spread, both)
        for c in range(across):
            rows, cols = slice(64 * g, 64 * (g + 1)), slice(c * LANES, (c + 1) * LANES)
            mask = mask_of(
                64 * g + iota((64, 1), 0), c * LANES + iota((1, LANES), 1)
            )
            tile = both[64 * c : 64 * (c + 1)]
            u_v[rows, cols] = tile[:, :LANES].astype(BF16)
            state_v[0, c // 2, rows, c % 2 * LANES : (c % 2 + 1) * LANES] = (
                tile[:, LANES:] * mask
            ).astype(BF16)

    loads[6].wait()
    wait_bytes(recv_sem, 3, left_mine)

    def build(s, carry):
        rotated = dot(left_v[s], u_v[...]).astype(BF16)
        built_v[s] = dot(u_v[...], rotated, ((0,), (0,))).astype(BF16)
        return carry

    lax.fori_loop(0, group, build, 0)

    def apply(s, carry):
        for side in range(2):
            applied_v[s, side] = dot(built_v[s], state_v[0, side]).astype(BF16)
        return carry

    lax.fori_loop(0, group, apply, 0)
    wait_bytes(recv_sem, 2, cbuf_v.at[pl.ds(0, pairs - group)])

    def mine_of(side):
        return pl.ds(pl.multiple_of(side * half, half), half)

    def meet_own(k):
        def one(s, carry):
            meet_v[s] = dot(state_v[k, core], comp_v[s, :, mine_of(core)], ((1,), (1,)))
            return carry

        lax.fori_loop(0, group, one, 0, unroll=True)

    def meet_other(k):
        def one(s, carry):
            met_v[s] = (
                meet_v[s]
                + dot(state_v[k, 1 - core], comp_v[s, :, mine_of(1 - core)], ((1,), (1,)))
            ).astype(BF16)
            return carry

        lax.fori_loop(0, group, one, 0, unroll=True)

    def rows_of(i):
        return pl.ds(pl.multiple_of(i * half, half), half)

    def later_term(i):
        total = dot(built_v[0, rows_of(i), :], met_v[0])
        for s in range(1, group):
            total += dot(built_v[s, rows_of(i), :], met_v[s])
        return total.astype(BF16)

    def first_term(i):
        total = jnp.zeros((half, half), F32)
        for s in range(group):
            for side in range(2):
                total += dot(
                    applied_v[s, side, rows_of(i), :],
                    comp_v[s, :, side * half : (side + 1) * half],
                    ((1,), (1,)),
                )
        return total.astype(BF16)

    def summed(slot):
        def some(j, carry):
            return carry + jnp.sum(rs_v[slot, pl.ds(j * 8, 8)].astype(F32), axis=0)

        return lax.fori_loop(0, chips // 8, some, jnp.zeros((ROWS, LANES), F32), unroll=True)

    mask = mask_of(
        lax.rem(chip, 2) * half + chip // 4 * ROWS + iota((ROWS, 1), 0),
        core * half + lax.rem(chip, 4) // 2 * LANES + iota((1, LANES), 1),
    )
    all_tiles = rs_v.at[0, pl.ds(0, chips - 1)]
    phase = 5
    pending = []
    for k in range(1, ORDER):
        slot = k - 1
        for j in range(2):
            parity = lax.rem(turn + j, 2)
            partial = first_term(parity) if k == 1 else later_term(parity)
            for c in range(2):
                part_v[parity, c] = partial[:, c * LANES : (c + 1) * LANES].reshape(
                    chips // 4, ROWS, LANES
                )
            send_half(phase, parity, rs_v.at[slot, chip])
        rs_v[slot, chip] = part_v[lax.rem(z, 2), lax.div(z, 2), lax.div(chip, 4)]
        factor = -(step_size / k)
        wait_bytes(recv_sem, phase, all_tiles)
        new = (factor * mask * summed(slot)).astype(BF16)
        tile_v[slot] = new
        state_v[k, core, term_rows, term_cols] = new
        send_chips(
            phase + 1, lambda q: tile_v.at[slot], state_v.at[(k, core, term_rows, term_cols)]
        )
        wait_bytes(send_sem, phase, all_tiles)
        wait_bytes(recv_sem, phase + 1, all_tiles)
        send(phase + 2, state_v.at[k, core], state_v.at[k, core], partner)
        meet_own(k)
        wait_bytes(recv_sem, phase + 2, state_v.at[k, 0])
        meet_other(k)
        pending += [(phase + 1, all_tiles), (phase + 2, state_v.at[0, 0])]
        phase += 3

    slot = ORDER - 1
    gather = (iota(square, 1) == gather_row(iota(square, 0))).astype(F32).astype(BF16)
    for i in range(2):
        upper = lax.rem(turn + i, 2)
        partial = later_term(upper)
        both = jnp.concatenate(
            [
                jnp.concatenate(
                    [
                        partial[128 * j : 128 * (j + 1), c * LANES : (c + 1) * LANES]
                        for c in range(2)
                    ],
                    axis=0,
                )
                for j in range(2)
            ],
            axis=1,
        )
        both = dot(gather, both).astype(BF16)
        for j in range(2):
            at_y = 2 * upper + j
            last_v[at_y] = both[:, j * LANES : (j + 1) * LANES].reshape(16, 16, LANES)
        for j in range(2):
            at_y = 2 * upper + j
            for a in (2, 1, 3, 0):
                for b in (2, 1, 3, 0):
                    device = (2 * at_y + core, to_n[a][b])
                    from_tile = last_v.at[at_y, to_n[a][b]]
                    if (a, b) == (0, 0):

                        @pl.when(y != at_y)
                        def _():
                            send(phase, from_tile, rs_v.at[slot, chip], device)

                    else:
                        send(phase, from_tile, rs_v.at[slot, chip], device)
    rs_v[slot, chip] = last_v[y, n]
    own_rows = states // parts
    pick = (iota((8, states), 1) == own_rows * me + iota((8, states), 0)).astype(F32).astype(BF16)
    so_far = []
    for side in range(2):
        total = dot(pick, state_v[0, side])
        for k in range(1, ORDER):
            total += dot(pick, state_v[k, side])
        so_far.append(total)
    wait_bytes(recv_sem, phase, all_tiles)
    total = summed(slot)
    pair_v[0] = total[:8]
    pair_v[1] = total[8:]
    send(phase + 1, pair_v.at[1 - core], pair_v.at[2 + core], partner)
    pair_v[2 + core] = pair_v[core]
    wait_bytes(send_sem, phase + 1, pair_v.at[0])
    wait_bytes(recv_sem, phase + 1, pair_v.at[0])
    for side in range(2):
        from_side = pair_v[2 + side]
        for c in range(2):
            cols = slice(side * half + c * LANES, side * half + (c + 1) * LANES)
            local = slice(c * LANES, (c + 1) * LANES)
            mask = mask_of(
                own_rows * me + iota((own_rows, 1), 0),
                side * half + c * LANES + iota((1, LANES), 1),
            )
            new = -(step_size / ORDER) * mask * from_side[own_rows * c : own_rows * (c + 1)]
            out_ref[:, cols] = so_far[side][:own_rows, local] + new.astype(BF16).astype(F32)

    wait_bytes(send_sem, 0, basis_all.at[0, pl.ds(0, 2 * plane - 2)])
    for started in (1, phases - 2):
        wait_bytes(send_sem, started, arrived)
    wait_bytes(send_sem, phases - 1, other_v)
    wait_bytes(send_sem, 2, recv_v.at[pl.ds(0, pairs - group)])
    wait_bytes(send_sem, 3, left_mine)
    wait_bytes(send_sem, 4, recv_v.at[pl.ds(0, 6 * plane)])
    wait_bytes(send_sem, phases - 3, basis_all.at[0])
    wait_bytes(send_sem, phases - 4, wave_all.at[0])
    for started, ref in pending:
        wait_bytes(send_sem, started, ref)
    wait_bytes(send_sem, phase, all_tiles)


def local(site_basis, left_ops, right_ops, integrals, wavefunction, pair_order, sector_sizes):
    states = wavefunction.shape[1]
    pairs = integrals.shape[0]
    per = left_ops.shape[0]
    parts = pairs // per
    vmem = pl.BlockSpec(memory_space=pltpu.VMEM)
    anywhere = pl.BlockSpec(memory_space=pltpu.HBM)
    ops = (2 * per, states, states)
    half = states // 2
    phases = 8 + 3 * ORDER
    body = lambda *refs: kernel(*refs, states=states, pairs=pairs, parts=parts)
    return pl.pallas_call(
        body,
        out_shape=jax.ShapeDtypeStruct(wavefunction.shape, F32),
        in_specs=[anywhere] * 7,
        out_specs=vmem,
        scratch_shapes=[
            pltpu.VMEM((1, pairs), jnp.int32),
            pltpu.SMEM(sector_sizes.shape, jnp.int32),
            pltpu.VMEM(site_basis.shape, BF16),
            pltpu.VMEM(integrals.shape, BF16),
            pltpu.VMEM(wavefunction.shape, BF16),
            pltpu.VMEM(ops, BF16),
            pltpu.VMEM((2, ROWS, LANES), BF16),
            pltpu.VMEM((2, parts // 2, ROWS, LANES), BF16),
            pltpu.VMEM((2, parts // 2, ROWS, LANES), BF16),
            pltpu.VMEM((states, states), BF16),
            pltpu.VMEM(ops, BF16),
            pltpu.VMEM((2 * per, 2, states, half), BF16),
            pltpu.VMEM((pairs, ROWS, LANES), BF16),
            pltpu.VMEM((2, pairs // 2, ROWS * LANES), BF16),
            pltpu.VMEM((pairs, ROWS * LANES), BF16),
            pltpu.VMEM((pairs, ROWS, LANES), BF16),
            pltpu.VMEM((2 * per, half, states), BF16),
            pltpu.VMEM((2, pairs, pairs // 2), BF16),
            pltpu.VMEM((ORDER, 2, states, half), BF16),
            pltpu.VMEM((2, 2, parts // 8, ROWS, LANES), BF16),
            pltpu.VMEM((ORDER, parts // 2, ROWS, LANES), BF16),
            pltpu.VMEM((4, parts // 8, ROWS, LANES), BF16),
            pltpu.VMEM((ORDER, ROWS, LANES), BF16),
            pltpu.VMEM((256, 256), BF16),
            pltpu.VMEM((4, 8, LANES), F32),
            pltpu.VMEM((per, half, states), BF16),
            pltpu.VMEM((pairs, ROWS * LANES), F32),
            pltpu.VMEM((2 * per, states, half), F32),
            pltpu.VMEM((2 * per, states, half), BF16),
            pltpu.SemaphoreType.DMA((7,)),
            pltpu.SemaphoreType.DMA((phases,)),
            pltpu.SemaphoreType.DMA((phases,)),
        ],
        compiler_params=pltpu.CompilerParams(
            collective_id=0, has_side_effects=True, vmem_limit_bytes=62 << 20
        ),
    )(
        pair_order.reshape(1, pairs), sector_sizes, site_basis, left_ops, right_ops,
        integrals, wavefunction,
    )


def solution(mesh):
    in_specs = (
        P(BOTH, None), P(BOTH, None, None), P(BOTH, None, None), P(), P(BOTH, None), P(), P()
    )
    return jax.shard_map(
        local, mesh=mesh, in_specs=in_specs, out_specs=P(BOTH, None), check_vma=False
    )
```

```python
import math

import jax
import jax.numpy as jnp
from jax import lax
from jax.experimental import pallas as pl
from jax.experimental.pallas import tpu as pltpu
from jax.sharding import PartitionSpec as P

ORDER = 3
ROWS, LANES = 16, 128
BF16, F32 = jnp.bfloat16, jnp.float32
BOTH = ("wide", "narrow")
MESH = pl.DeviceIdType.MESH


def dot(a, b, dims=((1,), (0,))):
    return lax.dot_general(a, b, (dims, ((), ())), preferred_element_type=F32)


def iota(shape, dim):
    return lax.broadcasted_iota(jnp.int32, shape, dim)


def tile_swap(size):
    o, m = iota((size, size), 0), iota((size, size), 1)
    return (m == (o & 15) * 16 + (o >> 4)).astype(F32).astype(BF16)


def spread_row(o):
    return ((o & 63) >> 2) * 16 + (o >> 6) * 4 + (o & 3)


def gather_row(o):
    return ((o >> 2) & 1) * 128 + ((o >> 3) & 1) * 64 + (o >> 4) * 4 + (o & 3)


def far_first(depth):
    steps = [
        (dy, dx, dz) for dy in range(4) for dx in range(4) for dz in range(depth)
    ]
    hops = lambda d: min(d[0], 4 - d[0]) + min(d[1], 4 - d[1])
    along_z = lambda d: min(d[2], 4 - d[2]) if depth == 4 else 2 * d[2]
    code = lambda d: d[0] * 16 + d[1] * 4 + d[2]
    back = lambda d: code([-i % 4 for i in d])
    pair = lambda d: (min(code(d), back(d)) * 37 % 64, code(d))
    return sorted(steps, key=lambda d: (-hops(d) - along_z(d), *pair(d)))


def kernel(
    order_ref, sizes_ref, basis_ref, left_ref, right_ref, integrals_ref, wave_ref,
    out_ref,
    order_v, sizes_v, basis_v, integrals_v, wave_v,
    left_v, pack_v, basis_all, wave_all, u_v, built_v, applied_v, recv_v, bm_v, ym_v, cbuf_v, comp_v,
    mix_v, state_v, part_v, rs_v, last_v, tile_v, swap_v, pair_v, other_v, acc_v, meet_v, met_v, local_sem, send_sem, recv_sem,
    *, states, pairs, parts,
):
    per = pairs // parts
    phases = 8 + 3 * ORDER
    group = 2 * per
    narrow = lax.axis_size("narrow")
    w, n = lax.axis_index("wide"), lax.axis_index("narrow")
    core = lax.rem(w, 2)
    me = w * narrow + n
    chips = parts // 2
    chip = w // 2 * narrow + n
    partner = (w + 1 - 2 * core, n)
    across = states // LANES
    half = states // 2
    step_size = 2.0 / math.sqrt(pairs)

    y, x, z = w // 2, n // 4, lax.rem(n, 4)

    to_w = [lax.rem(y + d, 4) * 2 + core for d in range(4)]
    to_y = [lax.rem(y + d, 4) * narrow for d in range(4)]
    to_x = [lax.rem(x + d, 4) * 4 for d in range(4)]
    to_z = [lax.rem(z + d, 4) for d in range(4)]

    def block(row, col):
        return (
            pl.ds(pl.multiple_of(row * ROWS, ROWS), ROWS),
            pl.ds(pl.multiple_of(col * LANES, LANES), LANES),
        )

    def mix_block(q):
        return block(lax.div(q, across), lax.rem(q, across))

    def term_block(q):
        return block(lax.rem(q, 2) * (chips // 4) + lax.div(q, 4), lax.div(lax.rem(q, 4), 2))

    def send(phase, src, dst, device):
        pltpu.make_async_remote_copy(
            src_ref=src, dst_ref=dst, send_sem=send_sem.at[phase],
            recv_sem=recv_sem.at[phase], device_id=device, device_id_type=MESH,
        ).start()

    to_n = [[i + j for j in to_z] for i in to_x]
    reached = [
        (to_y[dy] + to_n[dx][dz], (to_w[dy], to_n[dx][dz])) for dy, dx, dz in far_first(4)
    ]

    def each_chip(visit):
        for q, device in reached[:-1]:
            visit(q, device)

    def send_chips(phase, src, dst):
        each_chip(lambda q, device: send(phase, src(q), dst, device))

    turn = lax.rem(x + y + z, 2)

    def send_half(phase, parity, dst):
        first = lax.rem(parity + z, 2)
        at_z = [lax.rem(z + first + 2 * j, 4) for j in range(2)]
        half_z = [lax.div(j, 2) for j in at_z]
        at_yx = [[lax.div(i + j, 4) for j in to_x] for i in to_y]
        for dy, dx, dz in far_first(2):
            src = part_v.at[parity, half_z[dz], at_yx[dy][dx]]
            device = (to_w[dy], to_x[dx] + at_z[dz])
            if (dy, dx, dz) == (0, 0, 0):

                @pl.when(first == 1)
                def _():
                    send(phase, src, dst, device)

            else:
                send(phase, src, dst, device)

    def wait_bytes(sem, phase, ref):
        pltpu.make_async_copy(ref, ref, sem.at[phase]).wait()

    barrier = pltpu.get_barrier_semaphore()

    def greet(device):
        pl.semaphore_signal(barrier, inc=1, device_id=device, device_id_type=MESH)

    greet(partner)
    each_chip(lambda q, device: greet(device))
    half_rows = half // ROWS
    own_half = pl.ds(pl.multiple_of(core * half, half), half)
    other_half = pl.ds(pl.multiple_of((1 - core) * half, half), half)
    own_slots = pl.ds(core * (pairs // 2) + chip * per, per)
    other_slots = pl.ds((1 - core) * (pairs // 2) + chip * per, per)
    mix_rows, mix_cols = mix_block(chip)
    term_rows, term_cols = term_block(chip)
    loads = [
        pltpu.make_async_copy(src, dst, local_sem.at[i])
        for i, (src, dst) in enumerate(
            [
                (order_ref, order_v), (sizes_ref, sizes_v), (integrals_ref, integrals_v),
                (basis_ref, basis_v), (wave_ref, wave_v),
                (right_ref.at[:, block(core * half_rows + chip // across, 0)[0], mix_cols],
                 recv_v.at[own_slots]),
                (left_ref, left_v.at[pl.ds(core * per, per)]),
            ]
        )
    ]
    for load in loads:
        load.start()
    for load in loads[:5]:
        load.wait()

    def packed(ref):
        rows = ref[...].astype(F32)
        return jnp.concatenate(
            [rows[:, c * LANES : (c + 1) * LANES] for c in range(across)], axis=0
        ).astype(BF16)

    pack_v[0] = packed(basis_v)
    pack_v[1] = packed(wave_v)
    by_z = z * (chips // 4) + y * 4 + x
    basis_all[core, chip] = pack_v[0]
    wave_all[core, by_z] = pack_v[1]
    swap_v[...] = tile_swap(256)

    def take(ids, width):
        return (iota((pairs, width), 0) == ids).astype(F32).astype(BF16)

    def slot(of_chip, of_core, j):
        return ((of_chip // narrow * 2 + of_core) * narrow + (of_chip & (narrow - 1))) * per + j

    chosen = take(order_v[...], pairs)
    place = iota((1, pairs), 1)
    owner = (place * (65536 // group + 1)) >> 16
    rest = place - owner * group
    of_core = (rest >= per).astype(jnp.int32)
    order_of_owners = owner
    for i, (q, _) in enumerate(reached):
        owner = jnp.where(order_of_owners == i, q, owner)
    by_row = dot(chosen, take(slot(owner, of_core, rest - of_core * per), pairs)).astype(BF16)
    place = iota((1, pairs // 2), 1)
    sender = (place * (65536 // per + 1)) >> 16
    for c in range(2):
        by_column = dot(chosen, take(slot(sender, c, place - sender * per), pairs // 2))
        by_column = dot(integrals_v[...], by_column.astype(BF16)).astype(BF16)
        mix_v[c] = dot(by_row, by_column, ((0,), (0,))).astype(BF16)

    ends, total = [], jnp.int32(0)
    for b in range(sizes_ref.shape[0]):
        total = total + sizes_v[b]
        ends.append(total)

    def block_of(ids):
        found = jnp.zeros_like(ids)
        for end in ends:
            found = found + (ids >= end).astype(jnp.int32)
        return found

    def mask_of(row_ids, col_ids):
        return (jnp.abs(block_of(row_ids) - block_of(col_ids)) <= 2).astype(F32)

    pl.semaphore_wait(barrier, chips)

    send(phases - 1, right_ref.at[:, other_half, :], other_v, partner)
    for a in (2, 1, 3, 0):
        for b in (2, 1, 3, 0):
            if (a, b) != (0, 0):
                send(0, pack_v.at[0], basis_all.at[core, chip], (w, to_x[a] + to_z[b]))
                send(0, pack_v.at[1], wave_all.at[core, by_z], (to_w[a], to_x[b] + z))
    send_chips(
        1,
        lambda q: right_ref.at[
            (slice(None), *block(core * half_rows + lax.div(q, across), lax.rem(q, across)))
        ],
        recv_v.at[own_slots],
    )
    wait_bytes(recv_sem, phases - 1, other_v)
    send_chips(phases - 2, lambda q: other_v.at[(slice(None), *mix_block(q))], recv_v.at[other_slots])
    recv_v[other_slots] = other_v[:, mix_rows, mix_cols]
    plane = chips // 4
    wait_bytes(recv_sem, 0, basis_all.at[0, pl.ds(0, 2 * plane - 2)])
    for d in (2, 1, 3):
        block_of_y = basis_all.at[core, pl.ds(y * plane, plane)]
        send(4, block_of_y, block_of_y, (to_w[d], n))
        block_of_z = wave_all.at[core, pl.ds(z * plane, plane)]
        send(4, block_of_z, block_of_z, (w, to_x[0] + to_z[d]))
    left_mine = left_v.at[pl.ds(core * per, per)]
    send(3, left_ref, left_mine, partner)

    def into_rows(c):
        def some(q, carry):
            base = pl.multiple_of(q * 32, 32)
            both = jnp.concatenate(
                [
                    recv_v[pl.ds(c * (pairs // 2) + base + 16 * i, 16)].reshape(256, LANES)
                    for i in range(2)
                ],
                axis=1,
            )
            both = dot(swap_v[...], both).astype(BF16)
            for r in range(16):
                for i in range(2):
                    bm_v[c, pl.ds(base + 16 * i, 16), r * LANES : (r + 1) * LANES] = both[
                        16 * r : 16 * (r + 1), i * LANES : (i + 1) * LANES
                    ]
            return carry

        lax.fori_loop(0, pairs // 64, some, 0, unroll=True)

    def col_chunk(j):
        return pl.ds(pl.multiple_of(j * 256, 256), 256)

    arrived = recv_v.at[pl.ds(0, (chips - 1) * per)]
    loads[5].wait()
    wait_bytes(recv_sem, 1, arrived)
    into_rows(core)

    def mix_first(j, carry):
        acc_v[:, col_chunk(j)] = dot(mix_v[core], bm_v[core, :, col_chunk(j)])
        return carry

    lax.fori_loop(0, 8, mix_first, 0, unroll=True)
    wait_bytes(recv_sem, phases - 2, arrived)
    into_rows(1 - core)
    for begin, end in ((0, pairs // 4), (pairs // 4, pairs)):
        rows = slice(begin, end)

        def mix_second(j, carry, rows=rows):
            ym_v[rows, col_chunk(j)] = (
                acc_v[rows, col_chunk(j)]
                + dot(mix_v[1 - core, rows, :], bm_v[1 - core, :, col_chunk(j)])
            ).astype(BF16)
            return carry

        lax.fori_loop(0, 8, mix_second, 0, unroll=True)

        def into_tiles(q, carry, begin=begin):
            base = pl.multiple_of(q * 32 + begin, 32)
            both = jnp.concatenate(
                [
                    jnp.concatenate(
                        [
                            ym_v[pl.ds(base + 16 * j, 16), r * LANES : (r + 1) * LANES]
                            for r in range(16)
                        ],
                        axis=0,
                    )
                    for j in range(2)
                ],
                axis=1,
            )
            both = dot(swap_v[...], both).astype(BF16)
            for j in range(2):
                cbuf_v[pl.ds(base + 16 * j, 16)] = both[
                    :, j * LANES : (j + 1) * LANES
                ].reshape(16, 16, LANES)
            return carry

        lax.fori_loop(0, (end - begin) // 32, into_tiles, 0, unroll=True)
        for j in range(begin // group, min(end // group, chips - 1)):
            send(
                2,
                cbuf_v.at[pl.ds(j * group, group)],
                comp_v.at[:, mix_rows, mix_cols],
                reached[j][1],
            )
    comp_v[:, mix_rows, mix_cols] = cbuf_v[pairs - group :]

    wait_bytes(recv_sem, 4, recv_v.at[pl.ds(0, 6 * plane)])
    send(phases - 3, basis_all.at[core], basis_all.at[core], partner)
    send(phases - 4, wave_all.at[core], wave_all.at[core], partner)
    wait_bytes(recv_sem, phases - 3, basis_all.at[0])
    wait_bytes(recv_sem, phases - 4, wave_all.at[0])
    square = (256, 256)
    spread = (iota(square, 1) == spread_row(iota(square, 0))).astype(F32).astype(BF16)
    for g in range(states // 64):
        waves = [
            wave_all[g % 2, (i % 4) * plane + g // 2 * 4 + i // 4] for i in range(plane)
        ]
        both = jnp.concatenate(
            [
                basis_all[g % 2, g // 2 * plane : (g // 2 + 1) * plane].reshape(256, LANES),
                jnp.concatenate(waves, axis=0),
            ],
            axis=1,
        )
        both = dot(spread, both)
        for c in range(across):
            rows, cols = slice(64 * g, 64 * (g + 1)), slice(c * LANES, (c + 1) * LANES)
            mask = mask_of(
                64 * g + iota((64, 1), 0), c * LANES + iota((1, LANES), 1)
            )
            tile = both[64 * c : 64 * (c + 1)]
            u_v[rows, cols] = tile[:, :LANES].astype(BF16)
            state_v[0, c // 2, rows, c % 2 * LANES : (c % 2 + 1) * LANES] = (
                tile[:, LANES:] * mask
            ).astype(BF16)

    loads[6].wait()
    wait_bytes(recv_sem, 3, left_mine)

    def build(s, carry):
        rotated = dot(left_v[s], u_v[...]).astype(BF16)
        built_v[s] = dot(u_v[...], rotated, ((0,), (0,))).astype(BF16)
        return carry

    lax.fori_loop(0, group, build, 0)

    def apply(s, carry):
        for side in range(2):
            applied_v[s, side] = dot(built_v[s], state_v[0, side]).astype(BF16)
        return carry

    lax.fori_loop(0, group, apply, 0)
    wait_bytes(recv_sem, 2, cbuf_v.at[pl.ds(0, pairs - group)])

    def mine_of(side):
        return pl.ds(pl.multiple_of(side * half, half), half)

    def meet_own(k):
        def one(s, carry):
            meet_v[s] = dot(state_v[k, core], comp_v[s, :, mine_of(core)], ((1,), (1,)))
            return carry

        lax.fori_loop(0, group, one, 0, unroll=True)

    def meet_other(k):
        def one(s, carry):
            met_v[s] = (
                meet_v[s]
                + dot(state_v[k, 1 - core], comp_v[s, :, mine_of(1 - core)], ((1,), (1,)))
            ).astype(BF16)
            return carry

        lax.fori_loop(0, group, one, 0, unroll=True)

    def rows_of(i):
        return pl.ds(pl.multiple_of(i * half, half), half)

    def later_term(i):
        total = dot(built_v[0, rows_of(i), :], met_v[0])
        for s in range(1, group):
            total += dot(built_v[s, rows_of(i), :], met_v[s])
        return total.astype(BF16)

    def first_term(i):
        total = jnp.zeros((half, half), F32)
        for s in range(group):
            for side in range(2):
                total += dot(
                    applied_v[s, side, rows_of(i), :],
                    comp_v[s, :, side * half : (side + 1) * half],
                    ((1,), (1,)),
                )
        return total.astype(BF16)

    def summed(slot):
        def some(j, carry):
            return carry + jnp.sum(rs_v[slot, pl.ds(j * 8, 8)].astype(F32), axis=0)

        return lax.fori_loop(0, chips // 8, some, jnp.zeros((ROWS, LANES), F32), unroll=True)

    mask = mask_of(
        lax.rem(chip, 2) * half + chip // 4 * ROWS + iota((ROWS, 1), 0),
        core * half + lax.rem(chip, 4) // 2 * LANES + iota((1, LANES), 1),
    )
    all_tiles = rs_v.at[0, pl.ds(0, chips - 1)]
    phase = 5
    pending = []
    for k in range(1, ORDER):
        slot = k - 1
        for j in range(2):
            parity = lax.rem(turn + j, 2)
            partial = first_term(parity) if k == 1 else later_term(parity)
            for c in range(2):
                part_v[parity, c] = partial[:, c * LANES : (c + 1) * LANES].reshape(
                    chips // 4, ROWS, LANES
                )
            send_half(phase, parity, rs_v.at[slot, chip])
        rs_v[slot, chip] = part_v[lax.rem(z, 2), lax.div(z, 2), lax.div(chip, 4)]
        factor = -(step_size / k)
        wait_bytes(recv_sem, phase, all_tiles)
        new = (factor * mask * summed(slot)).astype(BF16)
        tile_v[slot] = new
        state_v[k, core, term_rows, term_cols] = new
        send_chips(
            phase + 1, lambda q: tile_v.at[slot], state_v.at[(k, core, term_rows, term_cols)]
        )
        wait_bytes(send_sem, phase, all_tiles)
        wait_bytes(recv_sem, phase + 1, all_tiles)
        send(phase + 2, state_v.at[k, core], state_v.at[k, core], partner)
        meet_own(k)
        wait_bytes(recv_sem, phase + 2, state_v.at[k, 0])
        meet_other(k)
        pending += [(phase + 1, all_tiles), (phase + 2, state_v.at[0, 0])]
        phase += 3

    slot = ORDER - 1
    gather = (iota(square, 1) == gather_row(iota(square, 0))).astype(F32).astype(BF16)
    for i in range(2):
        upper = lax.rem(turn + i, 2)
        partial = later_term(upper)
        both = jnp.concatenate(
            [
                jnp.concatenate(
                    [
                        partial[128 * j : 128 * (j + 1), c * LANES : (c + 1) * LANES]
                        for c in range(2)
                    ],
                    axis=0,
                )
                for j in range(2)
            ],
            axis=1,
        )
        both = dot(gather, both).astype(BF16)
        for j in range(2):
            at_y = 2 * upper + j
            last_v[at_y] = both[:, j * LANES : (j + 1) * LANES].reshape(16, 16, LANES)
        for j in range(2):
            at_y = 2 * upper + j
            for a in (2, 1, 3, 0):
                for b in (2, 1, 3, 0):
                    device = (2 * at_y + core, to_n[a][b])
                    from_tile = last_v.at[at_y, to_n[a][b]]
                    if (a, b) == (0, 0):

                        @pl.when(y != at_y)
                        def _():
                            send(phase, from_tile, rs_v.at[slot, chip], device)

                    else:
                        send(phase, from_tile, rs_v.at[slot, chip], device)
    rs_v[slot, chip] = last_v[y, n]
    own_rows = states // parts
    pick = (iota((8, states), 1) == own_rows * me + iota((8, states), 0)).astype(F32).astype(BF16)
    so_far = []
    for side in range(2):
        total = dot(pick, state_v[0, side])
        for k in range(1, ORDER):
            total += dot(pick, state_v[k, side])
        so_far.append(total)
    wait_bytes(recv_sem, phase, all_tiles)
    total = summed(slot)
    pair_v[0] = total[:8]
    pair_v[1] = total[8:]
    send(phase + 1, pair_v.at[1 - core], pair_v.at[2 + core], partner)
    pair_v[2 + core] = pair_v[core]
    wait_bytes(send_sem, phase + 1, pair_v.at[0])
    wait_bytes(recv_sem, phase + 1, pair_v.at[0])
    for side in range(2):
        from_side = pair_v[2 + side]
        for c in range(2):
            cols = slice(side * half + c * LANES, side * half + (c + 1) * LANES)
            local = slice(c * LANES, (c + 1) * LANES)
            mask = mask_of(
                own_rows * me + iota((own_rows, 1), 0),
                side * half + c * LANES + iota((1, LANES), 1),
            )
            new = -(step_size / ORDER) * mask * from_side[own_rows * c : own_rows * (c + 1)]
            out_ref[:, cols] = so_far[side][:own_rows, local] + new.astype(BF16).astype(F32)

    wait_bytes(send_sem, 0, basis_all.at[0, pl.ds(0, 2 * plane - 2)])
    for started in (1, phases - 2):
        wait_bytes(send_sem, started, arrived)
    wait_bytes(send_sem, phases - 1, other_v)
    wait_bytes(send_sem, 2, recv_v.at[pl.ds(0, pairs - group)])
    wait_bytes(send_sem, 3, left_mine)
    wait_bytes(send_sem, 4, recv_v.at[pl.ds(0, 6 * plane)])
    wait_bytes(send_sem, phases - 3, basis_all.at[0])
    wait_bytes(send_sem, phases - 4, wave_all.at[0])
    for started, ref in pending:
        wait_bytes(send_sem, started, ref)
    wait_bytes(send_sem, phase, all_tiles)


def local(site_basis, left_ops, right_ops, integrals, wavefunction, pair_order, sector_sizes):
    states = wavefunction.shape[1]
    pairs = integrals.shape[0]
    per = left_ops.shape[0]
    parts = pairs // per
    vmem = pl.BlockSpec(memory_space=pltpu.VMEM)
    anywhere = pl.BlockSpec(memory_space=pltpu.HBM)
    ops = (2 * per, states, states)
    half = states // 2
    phases = 8 + 3 * ORDER
    body = lambda *refs: kernel(*refs, states=states, pairs=pairs, parts=parts)
    return pl.pallas_call(
        body,
        out_shape=jax.ShapeDtypeStruct(wavefunction.shape, F32),
        in_specs=[anywhere] * 7,
        out_specs=vmem,
        scratch_shapes=[
            pltpu.VMEM((1, pairs), jnp.int32),
            pltpu.SMEM(sector_sizes.shape, jnp.int32),
            pltpu.VMEM(site_basis.shape, BF16),
            pltpu.VMEM(integrals.shape, BF16),
            pltpu.VMEM(wavefunction.shape, BF16),
            pltpu.VMEM(ops, BF16),
            pltpu.VMEM((2, ROWS, LANES), BF16),
            pltpu.VMEM((2, parts // 2, ROWS, LANES), BF16),
            pltpu.VMEM((2, parts // 2, ROWS, LANES), BF16),
            pltpu.VMEM((states, states), BF16),
            pltpu.VMEM(ops, BF16),
            pltpu.VMEM((2 * per, 2, states, half), BF16),
            pltpu.VMEM((pairs, ROWS, LANES), BF16),
            pltpu.VMEM((2, pairs // 2, ROWS * LANES), BF16),
            pltpu.VMEM((pairs, ROWS * LANES), BF16),
            pltpu.VMEM((pairs, ROWS, LANES), BF16),
            pltpu.VMEM((2 * per, half, states), BF16),
            pltpu.VMEM((2, pairs, pairs // 2), BF16),
            pltpu.VMEM((ORDER, 2, states, half), BF16),
            pltpu.VMEM((2, 2, parts // 8, ROWS, LANES), BF16),
            pltpu.VMEM((ORDER, parts // 2, ROWS, LANES), BF16),
            pltpu.VMEM((4, parts // 8, ROWS, LANES), BF16),
            pltpu.VMEM((ORDER, ROWS, LANES), BF16),
            pltpu.VMEM((256, 256), BF16),
            pltpu.VMEM((4, 8, LANES), F32),
            pltpu.VMEM((per, half, states), BF16),
            pltpu.VMEM((pairs, ROWS * LANES), F32),
            pltpu.VMEM((2 * per, states, half), F32),
            pltpu.VMEM((2 * per, states, half), BF16),
            pltpu.SemaphoreType.DMA((7,)),
            pltpu.SemaphoreType.DMA((phases,)),
            pltpu.SemaphoreType.DMA((phases,)),
        ],
        compiler_params=pltpu.CompilerParams(
            collective_id=0, has_side_effects=True,
            vmem_limit_bytes=62 << 20
        ),
    )(
        pair_order.reshape(1, pairs), sector_sizes, site_basis, left_ops, right_ops,
        integrals, wavefunction,
    )


def solution(mesh):
    in_specs = (
        P(BOTH, None), P(BOTH, None, None), P(BOTH, None, None), P(), P(BOTH, None), P(), P()
    )
    return jax.shard_map(
        local, mesh=mesh, in_specs=in_specs, out_specs=P(BOTH, None), check_vma=False
    )
```

```python
import math

import jax
import jax.numpy as jnp
from jax import lax
from jax.experimental import pallas as pl
from jax.experimental.pallas import tpu as pltpu
from jax.sharding import PartitionSpec as P

ORDER = 3
ROWS, LANES = 16, 128
BF16, F32 = jnp.bfloat16, jnp.float32
BOTH = ("wide", "narrow")
MESH = pl.DeviceIdType.MESH


def dot(a, b, dims=((1,), (0,))):
    return lax.dot_general(a, b, (dims, ((), ())), preferred_element_type=F32)


def iota(shape, dim):
    return lax.broadcasted_iota(jnp.int32, shape, dim)


def tile_swap(size):
    o, m = iota((size, size), 0), iota((size, size), 1)
    return (m == (o & 15) * 16 + (o >> 4)).astype(F32).astype(BF16)


def spread_row(o):
    return ((o & 63) >> 2) * 16 + (o >> 6) * 4 + (o & 3)


def gather_row(o):
    return ((o >> 2) & 1) * 128 + ((o >> 3) & 1) * 64 + (o >> 4) * 4 + (o & 3)


def far_first(depth):
    steps = [
        (dy, dx, dz) for dy in range(4) for dx in range(4) for dz in range(depth)
    ]
    hops = lambda d: min(d[0], 4 - d[0]) + min(d[1], 4 - d[1])
    along_z = lambda d: min(d[2], 4 - d[2]) if depth == 4 else 2 * d[2]
    code = lambda d: d[0] * 16 + d[1] * 4 + d[2]
    back = lambda d: code([-i % 4 for i in d])
    pair = lambda d: (min(code(d), back(d)) * 21 % 64, code(d))
    return sorted(steps, key=lambda d: (-hops(d) - along_z(d), *pair(d)))


def kernel(
    order_ref, sizes_ref, basis_ref, left_ref, right_ref, integrals_ref, wave_ref,
    out_ref,
    order_v, sizes_v, basis_v, integrals_v, wave_v,
    left_v, pack_v, basis_all, wave_all, u_v, built_v, applied_v, recv_v, bm_v, ym_v, cbuf_v, comp_v,
    mix_v, state_v, part_v, rs_v, last_v, tile_v, swap_v, pair_v, other_v, acc_v, meet_v, met_v, local_sem, send_sem, recv_sem,
    *, states, pairs, parts,
):
    per = pairs // parts
    phases = 8 + 3 * ORDER
    group = 2 * per
    narrow = lax.axis_size("narrow")
    w, n = lax.axis_index("wide"), lax.axis_index("narrow")
    core = lax.rem(w, 2)
    me = w * narrow + n
    chips = parts // 2
    chip = w // 2 * narrow + n
    partner = (w + 1 - 2 * core, n)
    across = states // LANES
    half = states // 2
    step_size = 2.0 / math.sqrt(pairs)

    y, x, z = w // 2, n // 4, lax.rem(n, 4)

    to_w = [lax.rem(y + d, 4) * 2 + core for d in range(4)]
    to_y = [lax.rem(y + d, 4) * narrow for d in range(4)]
    to_x = [lax.rem(x + d, 4) * 4 for d in range(4)]
    to_z = [lax.rem(z + d, 4) for d in range(4)]

    def block(row, col):
        return (
            pl.ds(pl.multiple_of(row * ROWS, ROWS), ROWS),
            pl.ds(pl.multiple_of(col * LANES, LANES), LANES),
        )

    def mix_block(q):
        return block(lax.div(q, across), lax.rem(q, across))

    def term_block(q):
        return block(lax.rem(q, 2) * (chips // 4) + lax.div(q, 4), lax.div(lax.rem(q, 4), 2))

    def send(phase, src, dst, device):
        pltpu.make_async_remote_copy(
            src_ref=src, dst_ref=dst, send_sem=send_sem.at[phase],
            recv_sem=recv_sem.at[phase], device_id=device, device_id_type=MESH,
        ).start()

    to_n = [[i + j for j in to_z] for i in to_x]
    reached = [
        (to_y[dy] + to_n[dx][dz], (to_w[dy], to_n[dx][dz])) for dy, dx, dz in far_first(4)
    ]

    def each_chip(visit):
        for q, device in reached[:-1]:
            visit(q, device)

    def send_chips(phase, src, dst):
        each_chip(lambda q, device: send(phase, src(q), dst, device))

    turn = lax.rem(x + y + z, 2)

    def send_half(phase, parity, dst):
        first = lax.rem(parity + z, 2)
        at_z = [lax.rem(z + first + 2 * j, 4) for j in range(2)]
        half_z = [lax.div(j, 2) for j in at_z]
        at_yx = [[lax.div(i + j, 4) for j in to_x] for i in to_y]
        for dy, dx, dz in far_first(2):
            src = part_v.at[parity, half_z[dz], at_yx[dy][dx]]
            device = (to_w[dy], to_x[dx] + at_z[dz])
            if (dy, dx, dz) == (0, 0, 0):

                @pl.when(first == 1)
                def _():
                    send(phase, src, dst, device)

            else:
                send(phase, src, dst, device)

    def wait_bytes(sem, phase, ref):
        pltpu.make_async_copy(ref, ref, sem.at[phase]).wait()

    barrier = pltpu.get_barrier_semaphore()

    def greet(device):
        pl.semaphore_signal(barrier, inc=1, device_id=device, device_id_type=MESH)

    greet(partner)
    each_chip(lambda q, device: greet(device))
    half_rows = half // ROWS
    own_half = pl.ds(pl.multiple_of(core * half, half), half)
    other_half = pl.ds(pl.multiple_of((1 - core) * half, half), half)
    own_slots = pl.ds(core * (pairs // 2) + chip * per, per)
    other_slots = pl.ds((1 - core) * (pairs // 2) + chip * per, per)
    mix_rows, mix_cols = mix_block(chip)
    term_rows, term_cols = term_block(chip)
    loads = [
        pltpu.make_async_copy(src, dst, local_sem.at[i])
        for i, (src, dst) in enumerate(
            [
                (order_ref, order_v), (sizes_ref, sizes_v), (integrals_ref, integrals_v),
                (basis_ref, basis_v), (wave_ref, wave_v),
                (right_ref.at[:, block(core * half_rows + chip // across, 0)[0], mix_cols],
                 recv_v.at[own_slots]),
                (left_ref, left_v.at[pl.ds(core * per, per)]),
            ]
        )
    ]
    for load in loads:
        load.start()
    for load in loads[:5]:
        load.wait()

    def packed(ref):
        rows = ref[...].astype(F32)
        return jnp.concatenate(
            [rows[:, c * LANES : (c + 1) * LANES] for c in range(across)], axis=0
        ).astype(BF16)

    pack_v[0] = packed(basis_v)
    pack_v[1] = packed(wave_v)
    by_z = z * (chips // 4) + y * 4 + x
    basis_all[core, chip] = pack_v[0]
    wave_all[core, by_z] = pack_v[1]
    swap_v[...] = tile_swap(256)

    def take(ids, width):
        return (iota((pairs, width), 0) == ids).astype(F32).astype(BF16)

    def slot(of_chip, of_core, j):
        return ((of_chip // narrow * 2 + of_core) * narrow + (of_chip & (narrow - 1))) * per + j

    chosen = take(order_v[...], pairs)
    place = iota((1, pairs), 1)
    owner = (place * (65536 // group + 1)) >> 16
    rest = place - owner * group
    of_core = (rest >= per).astype(jnp.int32)
    order_of_owners = owner
    for i, (q, _) in enumerate(reached):
        owner = jnp.where(order_of_owners == i, q, owner)
    by_row = dot(chosen, take(slot(owner, of_core, rest - of_core * per), pairs)).astype(BF16)
    place = iota((1, pairs // 2), 1)
    sender = (place * (65536 // per + 1)) >> 16
    for c in range(2):
        by_column = dot(chosen, take(slot(sender, c, place - sender * per), pairs // 2))
        by_column = dot(integrals_v[...], by_column.astype(BF16)).astype(BF16)
        mix_v[c] = dot(by_row, by_column, ((0,), (0,))).astype(BF16)

    ends, total = [], jnp.int32(0)
    for b in range(sizes_ref.shape[0]):
        total = total + sizes_v[b]
        ends.append(total)

    def block_of(ids):
        found = jnp.zeros_like(ids)
        for end in ends:
            found = found + (ids >= end).astype(jnp.int32)
        return found

    def mask_of(row_ids, col_ids):
        return (jnp.abs(block_of(row_ids) - block_of(col_ids)) <= 2).astype(F32)

    pl.semaphore_wait(barrier, chips)

    send(phases - 1, right_ref.at[:, other_half, :], other_v, partner)
    for a in (2, 1, 3, 0):
        for b in (2, 1, 3, 0):
            if (a, b) != (0, 0):
                send(0, pack_v.at[0], basis_all.at[core, chip], (w, to_x[a] + to_z[b]))
                send(0, pack_v.at[1], wave_all.at[core, by_z], (to_w[a], to_x[b] + z))
    send_chips(
        1,
        lambda q: right_ref.at[
            (slice(None), *block(core * half_rows + lax.div(q, across), lax.rem(q, across)))
        ],
        recv_v.at[own_slots],
    )
    wait_bytes(recv_sem, phases - 1, other_v)
    send_chips(phases - 2, lambda q: other_v.at[(slice(None), *mix_block(q))], recv_v.at[other_slots])
    recv_v[other_slots] = other_v[:, mix_rows, mix_cols]
    plane = chips // 4
    wait_bytes(recv_sem, 0, basis_all.at[0, pl.ds(0, 2 * plane - 2)])
    for d in (2, 1, 3):
        block_of_y = basis_all.at[core, pl.ds(y * plane, plane)]
        send(4, block_of_y, block_of_y, (to_w[d], n))
        block_of_z = wave_all.at[core, pl.ds(z * plane, plane)]
        send(4, block_of_z, block_of_z, (w, to_x[0] + to_z[d]))
    left_mine = left_v.at[pl.ds(core * per, per)]
    send(3, left_ref, left_mine, partner)

    def into_rows(c):
        def some(q, carry):
            base = pl.multiple_of(q * 32, 32)
            both = jnp.concatenate(
                [
                    recv_v[pl.ds(c * (pairs // 2) + base + 16 * i, 16)].reshape(256, LANES)
                    for i in range(2)
                ],
                axis=1,
            )
            both = dot(swap_v[...], both).astype(BF16)
            for r in range(16):
                for i in range(2):
                    bm_v[c, pl.ds(base + 16 * i, 16), r * LANES : (r + 1) * LANES] = both[
                        16 * r : 16 * (r + 1), i * LANES : (i + 1) * LANES
                    ]
            return carry

        lax.fori_loop(0, pairs // 64, some, 0, unroll=True)

    def col_chunk(j):
        return pl.ds(pl.multiple_of(j * 256, 256), 256)

    arrived = recv_v.at[pl.ds(0, (chips - 1) * per)]
    loads[5].wait()
    wait_bytes(recv_sem, 1, arrived)
    into_rows(core)

    def mix_first(j, carry):
        acc_v[:, col_chunk(j)] = dot(mix_v[core], bm_v[core, :, col_chunk(j)])
        return carry

    lax.fori_loop(0, 8, mix_first, 0, unroll=True)
    wait_bytes(recv_sem, phases - 2, arrived)
    into_rows(1 - core)
    for begin, end in ((0, pairs // 4), (pairs // 4, pairs)):
        rows = slice(begin, end)

        def mix_second(j, carry, rows=rows):
            ym_v[rows, col_chunk(j)] = (
                acc_v[rows, col_chunk(j)]
                + dot(mix_v[1 - core, rows, :], bm_v[1 - core, :, col_chunk(j)])
            ).astype(BF16)
            return carry

        lax.fori_loop(0, 8, mix_second, 0, unroll=True)

        def into_tiles(q, carry, begin=begin):
            base = pl.multiple_of(q * 32 + begin, 32)
            both = jnp.concatenate(
                [
                    jnp.concatenate(
                        [
                            ym_v[pl.ds(base + 16 * j, 16), r * LANES : (r + 1) * LANES]
                            for r in range(16)
                        ],
                        axis=0,
                    )
                    for j in range(2)
                ],
                axis=1,
            )
            both = dot(swap_v[...], both).astype(BF16)
            for j in range(2):
                cbuf_v[pl.ds(base + 16 * j, 16)] = both[
                    :, j * LANES : (j + 1) * LANES
                ].reshape(16, 16, LANES)
            return carry

        lax.fori_loop(0, (end - begin) // 32, into_tiles, 0, unroll=True)
        for j in range(begin // group, min(end // group, chips - 1)):
            send(
                2,
                cbuf_v.at[pl.ds(j * group, group)],
                comp_v.at[:, mix_rows, mix_cols],
                reached[j][1],
            )
    comp_v[:, mix_rows, mix_cols] = cbuf_v[pairs - group :]

    wait_bytes(recv_sem, 4, recv_v.at[pl.ds(0, 6 * plane)])
    send(phases - 3, basis_all.at[core], basis_all.at[core], partner)
    send(phases - 4, wave_all.at[core], wave_all.at[core], partner)
    wait_bytes(recv_sem, phases - 3, basis_all.at[0])
    wait_bytes(recv_sem, phases - 4, wave_all.at[0])
    square = (256, 256)
    spread = (iota(square, 1) == spread_row(iota(square, 0))).astype(F32).astype(BF16)
    for g in range(states // 64):
        waves = [
            wave_all[g % 2, (i % 4) * plane + g // 2 * 4 + i // 4] for i in range(plane)
        ]
        both = jnp.concatenate(
            [
                basis_all[g % 2, g // 2 * plane : (g // 2 + 1) * plane].reshape(256, LANES),
                jnp.concatenate(waves, axis=0),
            ],
            axis=1,
        )
        both = dot(spread, both)
        for c in range(across):
            rows, cols = slice(64 * g, 64 * (g + 1)), slice(c * LANES, (c + 1) * LANES)
            mask = mask_of(
                64 * g + iota((64, 1), 0), c * LANES + iota((1, LANES), 1)
            )
            tile = both[64 * c : 64 * (c + 1)]
            u_v[rows, cols] = tile[:, :LANES].astype(BF16)
            state_v[0, c // 2, rows, c % 2 * LANES : (c % 2 + 1) * LANES] = (
                tile[:, LANES:] * mask
            ).astype(BF16)

    loads[6].wait()
    wait_bytes(recv_sem, 3, left_mine)

    def build(s, carry):
        rotated = dot(left_v[s], u_v[...]).astype(BF16)
        built_v[s] = dot(u_v[...], rotated, ((0,), (0,))).astype(BF16)
        return carry

    lax.fori_loop(0, group, build, 0)

    def apply(s, carry):
        for side in range(2):
            applied_v[s, side] = dot(built_v[s], state_v[0, side]).astype(BF16)
        return carry

    lax.fori_loop(0, group, apply, 0)
    wait_bytes(recv_sem, 2, cbuf_v.at[pl.ds(0, pairs - group)])

    def mine_of(side):
        return pl.ds(pl.multiple_of(side * half, half), half)

    def meet_own(k):
        def one(s, carry):
            meet_v[s] = dot(state_v[k, core], comp_v[s, :, mine_of(core)], ((1,), (1,)))
            return carry

        lax.fori_loop(0, group, one, 0, unroll=True)

    def meet_other(k):
        def one(s, carry):
            met_v[s] = (
                meet_v[s]
                + dot(state_v[k, 1 - core], comp_v[s, :, mine_of(1 - core)], ((1,), (1,)))
            ).astype(BF16)
            return carry

        lax.fori_loop(0, group, one, 0, unroll=True)

    def rows_of(i):
        return pl.ds(pl.multiple_of(i * half, half), half)

    def later_term(i):
        total = dot(built_v[0, rows_of(i), :], met_v[0])
        for s in range(1, group):
            total += dot(built_v[s, rows_of(i), :], met_v[s])
        return total.astype(BF16)

    def first_term(i):
        total = jnp.zeros((half, half), F32)
        for s in range(group):
            for side in range(2):
                total += dot(
                    applied_v[s, side, rows_of(i), :],
                    comp_v[s, :, side * half : (side + 1) * half],
                    ((1,), (1,)),
                )
        return total.astype(BF16)

    def summed(slot):
        def some(j, carry):
            return carry + jnp.sum(rs_v[slot, pl.ds(j * 8, 8)].astype(F32), axis=0)

        return lax.fori_loop(0, chips // 8, some, jnp.zeros((ROWS, LANES), F32), unroll=True)

    mask = mask_of(
        lax.rem(chip, 2) * half + chip // 4 * ROWS + iota((ROWS, 1), 0),
        core * half + lax.rem(chip, 4) // 2 * LANES + iota((1, LANES), 1),
    )
    all_tiles = rs_v.at[0, pl.ds(0, chips - 1)]
    phase = 5
    pending = []
    for k in range(1, ORDER):
        slot = k - 1
        for j in range(2):
            parity = lax.rem(turn + j, 2)
            partial = first_term(parity) if k == 1 else later_term(parity)
            for c in range(2):
                part_v[parity, c] = partial[:, c * LANES : (c + 1) * LANES].reshape(
                    chips // 4, ROWS, LANES
                )
            send_half(phase, parity, rs_v.at[slot, chip])
        rs_v[slot, chip] = part_v[lax.rem(z, 2), lax.div(z, 2), lax.div(chip, 4)]
        factor = -(step_size / k)
        wait_bytes(recv_sem, phase, all_tiles)
        new = (factor * mask * summed(slot)).astype(BF16)
        tile_v[slot] = new
        state_v[k, core, term_rows, term_cols] = new
        send_chips(
            phase + 1, lambda q: tile_v.at[slot], state_v.at[(k, core, term_rows, term_cols)]
        )
        wait_bytes(send_sem, phase, all_tiles)
        wait_bytes(recv_sem, phase + 1, all_tiles)
        send(phase + 2, state_v.at[k, core], state_v.at[k, core], partner)
        meet_own(k)
        wait_bytes(recv_sem, phase + 2, state_v.at[k, 0])
        meet_other(k)
        pending += [(phase + 1, all_tiles), (phase + 2, state_v.at[0, 0])]
        phase += 3

    slot = ORDER - 1
    gather = (iota(square, 1) == gather_row(iota(square, 0))).astype(F32).astype(BF16)
    for i in range(2):
        upper = lax.rem(turn + i, 2)
        partial = later_term(upper)
        both = jnp.concatenate(
            [
                jnp.concatenate(
                    [
                        partial[128 * j : 128 * (j + 1), c * LANES : (c + 1) * LANES]
                        for c in range(2)
                    ],
                    axis=0,
                )
                for j in range(2)
            ],
            axis=1,
        )
        both = dot(gather, both).astype(BF16)
        for j in range(2):
            at_y = 2 * upper + j
            last_v[at_y] = both[:, j * LANES : (j + 1) * LANES].reshape(16, 16, LANES)
        for j in range(2):
            at_y = 2 * upper + j
            for a in (2, 1, 3, 0):
                for b in (2, 1, 3, 0):
                    device = (2 * at_y + core, to_n[a][b])
                    from_tile = last_v.at[at_y, to_n[a][b]]
                    if (a, b) == (0, 0):

                        @pl.when(y != at_y)
                        def _():
                            send(phase, from_tile, rs_v.at[slot, chip], device)

                    else:
                        send(phase, from_tile, rs_v.at[slot, chip], device)
    rs_v[slot, chip] = last_v[y, n]
    own_rows = states // parts
    pick = (iota((8, states), 1) == own_rows * me + iota((8, states), 0)).astype(F32).astype(BF16)
    so_far = []
    for side in range(2):
        total = dot(pick, state_v[0, side])
        for k in range(1, ORDER):
            total += dot(pick, state_v[k, side])
        so_far.append(total)
    wait_bytes(recv_sem, phase, all_tiles)
    total = summed(slot)
    pair_v[0] = total[:8]
    pair_v[1] = total[8:]
    send(phase + 1, pair_v.at[1 - core], pair_v.at[2 + core], partner)
    pair_v[2 + core] = pair_v[core]
    wait_bytes(send_sem, phase + 1, pair_v.at[0])
    wait_bytes(recv_sem, phase + 1, pair_v.at[0])
    for side in range(2):
        from_side = pair_v[2 + side]
        for c in range(2):
            cols = slice(side * half + c * LANES, side * half + (c + 1) * LANES)
            local = slice(c * LANES, (c + 1) * LANES)
            mask = mask_of(
                own_rows * me + iota((own_rows, 1), 0),
                side * half + c * LANES + iota((1, LANES), 1),
            )
            new = -(step_size / ORDER) * mask * from_side[own_rows * c : own_rows * (c + 1)]
            out_ref[:, cols] = so_far[side][:own_rows, local] + new.astype(BF16).astype(F32)

    wait_bytes(send_sem, 0, basis_all.at[0, pl.ds(0, 2 * plane - 2)])
    for started in (1, phases - 2):
        wait_bytes(send_sem, started, arrived)
    wait_bytes(send_sem, phases - 1, other_v)
    wait_bytes(send_sem, 2, recv_v.at[pl.ds(0, pairs - group)])
    wait_bytes(send_sem, 3, left_mine)
    wait_bytes(send_sem, 4, recv_v.at[pl.ds(0, 6 * plane)])
    wait_bytes(send_sem, phases - 3, basis_all.at[0])
    wait_bytes(send_sem, phases - 4, wave_all.at[0])
    for started, ref in pending:
        wait_bytes(send_sem, started, ref)
    wait_bytes(send_sem, phase, all_tiles)


def local(site_basis, left_ops, right_ops, integrals, wavefunction, pair_order, sector_sizes):
    states = wavefunction.shape[1]
    pairs = integrals.shape[0]
    per = left_ops.shape[0]
    parts = pairs // per
    vmem = pl.BlockSpec(memory_space=pltpu.VMEM)
    anywhere = pl.BlockSpec(memory_space=pltpu.HBM)
    ops = (2 * per, states, states)
    half = states // 2
    phases = 8 + 3 * ORDER
    body = lambda *refs: kernel(*refs, states=states, pairs=pairs, parts=parts)
    return pl.pallas_call(
        body,
        out_shape=jax.ShapeDtypeStruct(wavefunction.shape, F32),
        in_specs=[anywhere] * 7,
        out_specs=vmem,
        scratch_shapes=[
            pltpu.VMEM((1, pairs), jnp.int32),
            pltpu.SMEM(sector_sizes.shape, jnp.int32),
            pltpu.VMEM(site_basis.shape, BF16),
            pltpu.VMEM(integrals.shape, BF16),
            pltpu.VMEM(wavefunction.shape, BF16),
            pltpu.VMEM(ops, BF16),
            pltpu.VMEM((2, ROWS, LANES), BF16),
            pltpu.VMEM((2, parts // 2, ROWS, LANES), BF16),
            pltpu.VMEM((2, parts // 2, ROWS, LANES), BF16),
            pltpu.VMEM((states, states), BF16),
            pltpu.VMEM(ops, BF16),
            pltpu.VMEM((2 * per, 2, states, half), BF16),
            pltpu.VMEM((pairs, ROWS, LANES), BF16),
            pltpu.VMEM((2, pairs // 2, ROWS * LANES), BF16),
            pltpu.VMEM((pairs, ROWS * LANES), BF16),
            pltpu.VMEM((pairs, ROWS, LANES), BF16),
            pltpu.VMEM((2 * per, half, states), BF16),
            pltpu.VMEM((2, pairs, pairs // 2), BF16),
            pltpu.VMEM((ORDER, 2, states, half), BF16),
            pltpu.VMEM((2, 2, parts // 8, ROWS, LANES), BF16),
            pltpu.VMEM((ORDER, parts // 2, ROWS, LANES), BF16),
            pltpu.VMEM((4, parts // 8, ROWS, LANES), BF16),
            pltpu.VMEM((ORDER, ROWS, LANES), BF16),
            pltpu.VMEM((256, 256), BF16),
            pltpu.VMEM((4, 8, LANES), F32),
            pltpu.VMEM((per, half, states), BF16),
            pltpu.VMEM((pairs, ROWS * LANES), F32),
            pltpu.VMEM((2 * per, states, half), F32),
            pltpu.VMEM((2 * per, states, half), BF16),
            pltpu.SemaphoreType.DMA((7,)),
            pltpu.SemaphoreType.DMA((phases,)),
            pltpu.SemaphoreType.DMA((phases,)),
        ],
        compiler_params=pltpu.CompilerParams(
            collective_id=0, has_side_effects=True,
            vmem_limit_bytes=62 << 20
        ),
    )(
        pair_order.reshape(1, pairs), sector_sizes, site_basis, left_ops, right_ops,
        integrals, wavefunction,
    )


def solution(mesh):
    in_specs = (
        P(BOTH, None), P(BOTH, None, None), P(BOTH, None, None), P(), P(BOTH, None), P(), P()
    )
    return jax.shard_map(
        local, mesh=mesh, in_specs=in_specs, out_specs=P(BOTH, None), check_vma=False
    )
```
